32 devices in a mesh: dp: 8 (over z, core), context: 4 (over y, x).
Axes of the slice: x: 2, y: 2, z: 4, core: 2. Of those that a mesh axis runs over, the one named last changes fastest.
Arguments:
- layer_input: bfloat16 [8, 512, 8192], P('dp', 'context'), may hold values from -150 to 150
- value_weight: bfloat16 [8192, 512], replicated, may hold values from -0.0625 to 0.0625
- queries: bfloat16 [8, 512, 4096], P('dp', 'context'), may hold values from -150 to 150
- key_states: bfloat16 [8, 512, 512], P('dp', 'context'), may hold values from -6 to 6
- out_grads: bfloat16 [8, 512, 4096], P('dp', 'context'), may hold values from -16 to 16
- lengths: int32 [8], P('dp'), may hold values from 0 to 512, as said below
Outputs:
- clipped_sum: float32 [8192, 512], P('context', 'dp')
- doc_norms: float32 [8], P('dp')
- key_grads: bfloat16 [8, 512, 512], P('dp', 'context')
The draws below stay inside these ranges and needn't reach their ends.
Inputs may be any that keep to these rules, and one draw needn't show every extreme that they name: `lengths`: a slot's document fills the slot's first positions; in every draw some slot is empty and some slot is full.
All inputs are finite; a program needn't handle non-finite values.
Results may differ from the reference program's by a relative error of at most 0.02.
Values may be sent and summed in bfloat16 or wider, within the bound.
No kernel may reach another device: no remote copies, remote signals or barrier semaphores. Data moves between devices by JAX's collectives and lax.ppermute only.
A program may use at most 128 MiB of HBM per device.

```python
import math
import jax
import jax.numpy as jnp
from jax import lax

D = 8192
HD = 128
QH = 32
KVH = 4
SEQ = 512
SLOTS = 8


def query_key_pair(key):
    seeds = jax.random.split(jax.random.fold_in(key, 7101), 2)
    key_shape = (SLOTS, SEQ, KVH, HD)
    query_shape = (SLOTS, SEQ, QH, HD)
    key_values = jnp.clip(jax.random.normal(seeds[0], key_shape, jnp.float32), -5.0, 5.0)
    query_values = jnp.clip(jax.random.normal(seeds[1], query_shape, jnp.float32), -5.0, 5.0)
    return (query_values.reshape(SLOTS, SEQ, QH * HD), key_values.reshape(SLOTS, SEQ, KVH * HD))


def draw_queries(key, part):
    return query_key_pair(key)[0].astype(jnp.bfloat16)


def draw_key_states(key, part):
    return query_key_pair(key)[1].astype(jnp.bfloat16)


def draw_layer_input(key, part):
    seeds = jax.random.split(jax.random.fold_in(key, 3301), 3)
    position_ramp = 0.6 * 3.0 ** (jnp.arange(SEQ, dtype=jnp.float32) / max(SEQ - 1, 1))
    feature_ramp = 0.6 * 3.0 ** (jnp.arange(D, dtype=jnp.float32) / (D - 1))
    row_scale = jnp.exp(jax.random.uniform(seeds[0], (SLOTS, SEQ, 1), jnp.float32, math.log(0.3), math.log(3.0)))
    row_scale = row_scale * position_ramp[None, :, None]
    column_scale = jnp.exp(jax.random.uniform(seeds[1], (SLOTS, 1, D), jnp.float32, math.log(0.3), math.log(3.0)))
    column_scale = column_scale * feature_ramp[None, None, :]
    base_values = jnp.clip(jax.random.normal(seeds[2], (SLOTS, SEQ, D), jnp.float32), -4.0, 4.0)
    return (base_values * row_scale * column_scale).astype(jnp.bfloat16)


def draw_out_grads(key, part):
    seeds = jax.random.split(jax.random.fold_in(key, 4401), 2)
    width = QH * HD
    column_scale = jnp.exp(jax.random.uniform(seeds[0], (SLOTS, 1, width), jnp.float32, math.log(0.3), math.log(3.0)))
    base_values = jnp.clip(jax.random.normal(seeds[1], (SLOTS, SEQ, width), jnp.float32), -4.0, 4.0)
    return (base_values * column_scale).astype(jnp.bfloat16)


def draw_lengths(key, part):
    seeds = jax.random.split(jax.random.fold_in(key, 5501), 3)
    base_values = jax.random.randint(seeds[0], (SLOTS,), SEQ // 8, SEQ + 1, dtype=jnp.int32)
    empty = jax.random.randint(seeds[1], (SLOTS,), 0, 4, dtype=jnp.int32) == 0
    base_values = jnp.where(empty, jnp.zeros_like(base_values), base_values)
    shuffled = jax.random.permutation(seeds[2], SLOTS)
    slot_index = jnp.arange(SLOTS, dtype=jnp.int32)
    base_values = jnp.where(slot_index == shuffled[0], SEQ, base_values)
    base_values = jnp.where(slot_index == shuffled[1], 0, base_values)
    return base_values.astype(jnp.int32)


def centred(key, extent, scale, bound, held_as=jnp.bfloat16):
    return jnp.clip(scale * jax.random.normal(key, extent, jnp.float32), -bound, bound).astype(held_as)


def setup_inputs(seed: int = 0) -> dict:
    keys = jax.random.split(jax.random.key(seed), 7)
    return {
        "layer_input": draw_layer_input(jax.random.fold_in(keys[6], 71), 0),
        "value_weight": centred(keys[1], (D, KVH * HD), D ** -0.5, 0.0625),
        "queries": draw_queries(jax.random.fold_in(keys[6], 71), 0),
        "key_states": draw_key_states(jax.random.fold_in(keys[6], 71), 0),
        "out_grads": draw_out_grads(jax.random.fold_in(keys[6], 71), 0),
        "lengths": draw_lengths(jax.random.fold_in(keys[6], 71), 0),
    }


def head_grads(query_rows, grad_rows, key_rows, value_rows, causal, softmax_scale):
    scores = jnp.dot(query_rows, key_rows.T, preferred_element_type=jnp.float32) * softmax_scale
    scores = jnp.where(causal, scores, -jnp.inf)
    row_peak = lax.optimization_barrier(jnp.max(scores, axis=-1, keepdims=True))
    weights = jnp.exp(scores - row_peak)
    weights = weights / lax.optimization_barrier(jnp.sum(weights, axis=-1, keepdims=True))
    probs_low = weights.astype(jnp.bfloat16)
    attended = jnp.dot(probs_low, value_rows, preferred_element_type=jnp.float32)
    offsets = lax.optimization_barrier(jnp.sum(grad_rows.astype(jnp.float32) * attended, axis=-1))
    grad_probs = jnp.dot(grad_rows, value_rows.T, preferred_element_type=jnp.float32)
    grad_scores = (weights * (grad_probs - offsets[:, None])).astype(jnp.bfloat16)
    key_part = jnp.dot(grad_scores.T, query_rows, preferred_element_type=jnp.float32) * softmax_scale
    value_part = jnp.dot(probs_low.T, grad_rows, preferred_element_type=jnp.float32)
    return (key_part, value_part)

def reference(layer_input, value_weight, queries, key_states, out_grads, lengths):
    softmax_scale = HD ** (-0.5)
    positions = jnp.arange(SEQ, dtype=jnp.int32)
    causal = positions[:, None] >= positions[None, :]
    clip_norm = math.sqrt(D * KVH * HD)

    def one_slot(running, slot_data):
        input_doc, query_doc, key_doc, grad_doc, length = slot_data
        value_doc = jnp.dot(input_doc, value_weight, preferred_element_type=jnp.float32).astype(jnp.bfloat16)
        grad_doc = jnp.where((positions < length)[:, None], grad_doc, jnp.zeros_like(grad_doc))
        query_heads = query_doc.reshape(SEQ, QH, HD).transpose(1, 0, 2)
        grad_heads = grad_doc.reshape(SEQ, QH, HD).transpose(1, 0, 2)
        key_heads = jnp.repeat(key_doc.reshape(SEQ, KVH, HD).transpose(1, 0, 2), QH // KVH, axis=0)
        value_heads = jnp.repeat(value_doc.reshape(SEQ, KVH, HD).transpose(1, 0, 2), QH // KVH, axis=0)

        def one_head(head_data):
            return head_grads(head_data[0], head_data[1], head_data[2], head_data[3], causal, softmax_scale)
        key_parts, value_parts = lax.map(one_head, (query_heads, grad_heads, key_heads, value_heads))
        key_sum = key_parts.reshape(KVH, QH // KVH, SEQ, HD).sum(axis=1).transpose(1, 0, 2).reshape(SEQ, KVH * HD)
        value_sum = value_parts.reshape(KVH, QH // KVH, SEQ, HD).sum(axis=1).transpose(1, 0, 2).reshape(SEQ, KVH * HD)
        value_low = value_sum.astype(jnp.bfloat16)
        doc_grad = jnp.dot(input_doc.T, value_low, preferred_element_type=jnp.float32)
        doc_norm = jnp.sqrt(jnp.sum(doc_grad * doc_grad))
        running = running + doc_grad * (clip_norm / (doc_norm + 0.01))
        return (running, (doc_norm, key_sum.astype(jnp.bfloat16)))
    running_sum = jnp.zeros((D, KVH * HD), jnp.float32)
    clipped_sum, (doc_norms, key_grads) = lax.scan(one_slot, running_sum, (layer_input, queries, key_states, out_grads, lengths))
    return (clipped_sum, doc_norms, key_grads)
```

```python
import functools
import math

import jax
import jax.numpy as jnp
from jax import lax
from jax.experimental import pallas as pl
from jax.experimental.pallas import tpu as pltpu
from jax.sharding import PartitionSpec as P

HD = 128
BOTH = ("dp", "context")
CHUNKS = 4
F32 = jnp.float32
BF16 = jnp.bfloat16


NT = (((1,), (1,)), ((), ()))
TN = (((0,), (0,)), ((), ()))


def estimate(flops, nbytes, exps=0):
    return pl.CostEstimate(flops=flops, bytes_accessed=nbytes, transcendentals=exps)


def project(place, layer_rows, value_weight, parts, chunks):
    rows, width = layer_rows.shape
    cols = value_weight.shape[1]
    own = width // parts
    piece = own // chunks

    def kernel(place_ref, x_ref, w_ref, v_ref, *rest):
        outs, acc_ref = rest[:-1], rest[-1]
        step = pl.program_id(0)
        part = jnp.dot(x_ref[...], w_ref[...], preferred_element_type=F32)

        @pl.when(step == 0)
        def _():
            acc_ref[...] = part

        @pl.when(step > 0)
        def _():
            acc_ref[...] += part

        for k in range(parts):

            @pl.when(step == k)
            def _(k=k):
                for j in range(chunks):
                    outs[k * chunks + j][...] = x_ref[:, j * piece : (j + 1) * piece]

        @pl.when(step == parts - 1)
        def _():
            v_ref[...] = acc_ref[...].astype(BF16)

    whole = lambda shape: pl.BlockSpec(shape, lambda k, p: (0, 0))
    out = pl.pallas_call(
        kernel,
        out_shape=[jax.ShapeDtypeStruct((rows, cols), BF16)]
        + [jax.ShapeDtypeStruct((rows, piece), BF16)] * (parts * chunks),
        grid_spec=pltpu.PrefetchScalarGridSpec(
            num_scalar_prefetch=1,
            grid=(parts,),
            in_specs=[
                pl.BlockSpec((rows, own), lambda k, p: (0, p[0] ^ k)),
                pl.BlockSpec((own, cols), lambda k, p: (p[0] ^ k, 0)),
            ],
            out_specs=[whole((rows, cols))] + [whole((rows, piece))] * (parts * chunks),
            scratch_shapes=[pltpu.VMEM((rows, cols), F32)],
        ),
        compiler_params=pltpu.CompilerParams(dimension_semantics=("arbitrary",)),
        cost_estimate=estimate(2 * rows * width * cols, 2 * (width * cols + 2 * rows * width)),
        name="project",
    )(place, layer_rows, value_weight)
    pieces = out[1:]
    return out[0], [[pieces[k * chunks + j] for j in range(chunks)] for k in range(parts)]


def attend(place, queries, out_grads, keys, values):
    rows, width = queries.shape
    parts = len(keys)
    kv_width = keys[0].shape[1]
    groups = kv_width // HD
    per_group = width // HD // groups
    span = per_group * HD
    total = rows * parts
    scale = HD ** (-0.5)

    def kernel(place_ref, q_ref, o_ref, *rest):
        k_refs, v_refs = rest[:parts], rest[parts : 2 * parts]
        dk_refs, dv_refs = rest[2 * parts : 3 * parts], rest[3 * parts : 4 * parts]
        p_buf, s_buf, q_buf, o_buf = rest[4 * parts :]
        me, length = place_ref[0], place_ref[1]
        key_rows = jnp.concatenate([r[...] for r in k_refs], axis=0)
        value_rows = jnp.concatenate([r[...] for r in v_refs], axis=0)
        local = lax.broadcasted_iota(jnp.int32, (rows, rows), 0)
        lane = lax.broadcasted_iota(jnp.int32, (rows, rows), 1)
        base = me * rows
        keep = [(me ^ k) * rows + local <= base + lane for k in range(parts)]
        keep = jnp.concatenate(keep, axis=0)
        valid = base + lax.broadcasted_iota(jnp.int32, (rows, HD), 0) < length
        for h in range(per_group):
            cols = slice(h * HD, (h + 1) * HD)
            q = q_ref[:, cols]
            o = o_ref[:, cols]
            o = jnp.where(valid, o, jnp.zeros_like(o))
            q_buf[h * rows : (h + 1) * rows, :] = q
            o_buf[h * rows : (h + 1) * rows, :] = o
            s = lax.dot_general(key_rows, q, NT, preferred_element_type=F32)
            s = jnp.where(keep, s * scale, -jnp.inf)
            p = jnp.exp(s - jnp.max(s, axis=0, keepdims=True))
            p = p * (1.0 / jnp.sum(p, axis=0, keepdims=True))
            low = p.astype(BF16)
            g = lax.dot_general(value_rows, o, NT, preferred_element_type=F32)
            offset = jnp.sum(low.astype(F32) * g, axis=0, keepdims=True)
            p_buf[:, h * rows : (h + 1) * rows] = low
            s_buf[:, h * rows : (h + 1) * rows] = (p * (g - offset)).astype(BF16)
        dk = jnp.dot(s_buf[...], q_buf[...], preferred_element_type=F32) * scale
        dv = jnp.dot(p_buf[...], o_buf[...], preferred_element_type=F32)
        for k in range(parts):
            block = slice(k * rows, (k + 1) * rows)
            dk_refs[k][...] = dk[block].astype(dk_refs[k].dtype)
            dv_refs[k][...] = dv[block].astype(dv_refs[k].dtype)

    wide = pl.BlockSpec((rows, span), lambda g, p: (0, g))
    narrow = pl.BlockSpec((rows, HD), lambda g, p: (0, g))
    kinds = [F32] + [BF16] * (parts - 1)
    shapes = [jax.ShapeDtypeStruct((rows, kv_width), kind) for kind in kinds]
    out = pl.pallas_call(
        kernel,
        out_shape=shapes * 2,
        grid_spec=pltpu.PrefetchScalarGridSpec(
            num_scalar_prefetch=1,
            grid=(groups,),
            in_specs=[wide, wide] + [narrow] * (2 * parts),
            out_specs=[narrow] * (2 * parts),
            scratch_shapes=[
                pltpu.VMEM((total, per_group * rows), BF16),
                pltpu.VMEM((total, per_group * rows), BF16),
                pltpu.VMEM((per_group * rows, HD), BF16),
                pltpu.VMEM((per_group * rows, HD), BF16),
            ],
        ),
        compiler_params=pltpu.CompilerParams(dimension_semantics=("arbitrary",)),
        cost_estimate=estimate(
            10 * rows * total * width, 2 * (2 * rows * width + 4 * total * kv_width), rows * total * width // HD
        ),
        name="attend",
    )(place, queries, out_grads, *keys, *values)
    return out[:parts], out[parts:]


def doc_grad(place, value_grads, features, blocks):
    parts = len(features)
    rows, chunk = features[0].shape
    cols = value_grads[0].shape[1]
    width = cols // blocks
    half = blocks // 2

    def kernel(place_ref, *refs):
        x_refs, d_refs = refs[:parts], refs[parts : 2 * parts]
        keep_ref, send_ref, square_ref, flip = refs[2 * parts :]
        odd = place_ref[2]
        grads = jnp.concatenate([r[...] for r in d_refs], axis=0)
        flip[...] = grads.T
        x = jnp.concatenate([r[...] for r in x_refs], axis=0)

        def side(which):
            picked = [
                flip[pl.ds(pl.multiple_of((2 * z + which) * width, width), width), :] for z in range(half)
            ]
            return jnp.dot(jnp.concatenate(picked, axis=0), x, preferred_element_type=F32)

        kept = side(odd)
        sent = side(1 - odd)
        keep_ref[...] = kept
        send_ref[...] = sent.astype(BF16)
        both = kept * kept + sent * sent
        folded = jnp.sum(both.reshape(half * width // 8, 8, chunk), axis=0)
        square_ref[...] = sum(folded[:, i * HD : (i + 1) * HD] for i in range(chunk // HD))

    vmem = pl.BlockSpec(memory_space=pltpu.VMEM)
    return pl.pallas_call(
        kernel,
        out_shape=[
            jax.ShapeDtypeStruct((half * width, chunk), F32),
            jax.ShapeDtypeStruct((half * width, chunk), BF16),
            jax.ShapeDtypeStruct((8, HD), F32),
        ],
        in_specs=[pl.BlockSpec(memory_space=pltpu.SMEM)] + [vmem] * (2 * parts),
        out_specs=[vmem] * 3,
        scratch_shapes=[pltpu.VMEM((cols, rows * parts), BF16)],
        cost_estimate=estimate(2 * rows * parts * chunk * cols, 2 * rows * parts * (chunk + cols) + 3 * cols * chunk),
        name="doc_grad",
    )(place, *features, *value_grads)


def combine(place, squares, kept, received, blocks, clip):
    half = blocks // 2
    tall, chunk = kept[0].shape
    width = tall // half
    chunks = len(kept)
    count = len(squares)

    def kernel(place_ref, *refs):
        square_refs = refs[:count]
        keep_refs = refs[count : count + chunks]
        got_refs = refs[count + chunks : count + 2 * chunks]
        norm_ref, outs = refs[count + 2 * chunks], refs[count + 2 * chunks + 1 :]
        z = place_ref[3]
        sums = square_refs[0][...]
        for r in square_refs[1:]:
            sums = sums + r[...]

        def norm(block):
            lanes = jnp.sum(block, axis=1, keepdims=True)
            return jnp.sqrt(jnp.sum(lanes, axis=0, keepdims=True))

        mine, other = norm(sums[:8]), norm(sums[8:])
        norm_ref[...] = jnp.broadcast_to(mine, (8, HD))
        mine, other = clip / (mine + 0.01), clip / (other + 0.01)
        for k in range(half):
            rows = pl.ds(pl.multiple_of((z ^ k) * width, width), width)
            for j in range(chunks):
                total = keep_refs[j][rows, :] * mine + got_refs[j][rows, :].astype(F32) * other
                outs[k][:, j * chunk : (j + 1) * chunk] = total.astype(BF16)

    vmem = pl.BlockSpec(memory_space=pltpu.VMEM)
    out = pl.pallas_call(
        kernel,
        out_shape=[jax.ShapeDtypeStruct((8, HD), F32)]
        + [jax.ShapeDtypeStruct((width, chunk * chunks), BF16)] * half,
        in_specs=[pl.BlockSpec(memory_space=pltpu.SMEM)] + [vmem] * (count + 2 * chunks),
        out_specs=[vmem] * (half + 1),
        cost_estimate=estimate(4 * tall * chunk * chunks, 8 * tall * chunk * chunks),
        name="combine",
    )(place, *squares, *kept, *received)
    return out[0], out[1:]


def body(layer_input, value_weight, queries, key_states, out_grads, lengths):
    parts = lax.axis_size("context")
    docs = lax.axis_size("dp")
    planes = docs // 2
    context = lax.axis_index("context")
    doc = lax.axis_index("dp")
    place = jnp.stack([context, lengths[0], doc % 2, doc // 2]).astype(jnp.int32)
    rows = layer_input.shape[1]
    width = layer_input.shape[2]
    cols = value_weight.shape[1]

    def over_context(x, k):
        return lax.ppermute(x, "context", [(i, i ^ k) for i in range(parts)])

    def over_planes(x, k):
        return lax.ppermute(x, "dp", [(i, i ^ (2 * k)) for i in range(docs)])

    def over_cores(x):
        return lax.ppermute(x, "dp", [(i, i ^ 1) for i in range(docs)])

    keys = [key_states[0]] + [over_context(key_states[0], k) for k in range(1, parts)]
    own_values, pieces = project(place, layer_input[0], value_weight, parts, CHUNKS)
    values = [own_values] + [over_context(own_values, k) for k in range(1, parts)]
    features = []
    for j in range(CHUNKS):
        features.append([pieces[0][j]] + [over_context(pieces[k][j], k) for k in range(1, parts)])

    key_parts, value_parts = attend(place, queries[0], out_grads[0], keys, values)

    value_sum = value_parts[0]
    for k in range(1, parts):
        value_sum = value_sum + over_context(value_parts[k], k).astype(F32)
    value_low = value_sum.astype(BF16)
    value_grads = [value_low] + [over_context(value_low, k) for k in range(1, parts)]

    key_sum = key_parts[0]
    for k in range(1, parts):
        key_sum = key_sum + over_context(key_parts[k], k).astype(F32)
    key_grads = key_sum.astype(BF16)[None]

    kept, received, squares = [], [], 0.0
    for j in range(CHUNKS):
        keep, send, square = doc_grad(place, value_grads, features[j], docs)
        kept.append(keep)
        received.append(over_cores(send))
        squares = squares + square
    squares = jnp.concatenate([squares, over_cores(squares)], axis=0)
    squares = [squares] + [over_context(squares, k) for k in range(1, parts)]
    norm, shares = combine(place, squares, kept, received, docs, math.sqrt(width * cols))
    total = shares[0].astype(F32)
    for k in range(1, planes):
        total = total + over_planes(shares[k], k).astype(F32)
    return total.T, norm[0, :1], key_grads


def solution(mesh):
    placed = (
        P("dp", "context", None),
        P(),
        P("dp", "context", None),
        P("dp", "context", None),
        P("dp", "context", None),
        P("dp"),
    )
    return jax.shard_map(
        body,
        mesh=mesh,
        in_specs=placed,
        out_specs=(P("context", "dp"), P("dp"), P("dp", "context", None)),
        check_vma=False,
    )
```

```python
import math

import jax
import jax.numpy as jnp
from jax import lax
from jax.experimental import pallas as pl
from jax.experimental.pallas import tpu as pltpu
from jax.sharding import PartitionSpec as P

HD = 128
LANES = 128
FIRST_SHARE = 10
HEAVY = 10
F32 = jnp.float32
BF16 = jnp.bfloat16
LOG2E = 1.4426950408889634


NT = (((1,), (1,)), ((), ()))
VMEM = pl.BlockSpec(memory_space=pltpu.VMEM)
SMEM = pl.BlockSpec(memory_space=pltpu.SMEM)


def estimate(flops, nbytes, exps=0):
    return pl.CostEstimate(flops=flops, bytes_accessed=nbytes, transcendentals=exps)


def grant(mib):
    return pltpu.CompilerParams(vmem_limit_bytes=mib << 20)


def split(own):
    units = own // LANES
    first = max(1, units * FIRST_SHARE // 16)
    return [first * LANES, (units - first) * LANES]


def cut(place, layer_rows, parts, sizes):
    rows, width = layer_rows.shape
    own = width // parts
    chunks = len(sizes)

    def kernel(place_ref, x_ref, *outs):
        for k in range(parts):
            start = (place_ref[0] ^ k) * own
            for j in range(chunks):
                span = pl.ds(pl.multiple_of(start + sum(sizes[:j]), LANES), sizes[j])
                outs[k * chunks + j][...] = x_ref[:, span]

    out = pl.pallas_call(
        kernel,
        out_shape=[jax.ShapeDtypeStruct((rows, size), BF16) for _ in range(parts) for size in sizes],
        in_specs=[SMEM, VMEM],
        out_specs=[VMEM] * (parts * chunks),
        compiler_params=grant(8),
        cost_estimate=estimate(0, HEAVY * 4 * rows * width),
        name="cut",
    )(place, layer_rows)
    return [[out[k * chunks + j] for j in range(chunks)] for k in range(parts)]


def project(layer_rows, value_weight):
    rows, width = layer_rows.shape
    cols = value_weight.shape[1]
    depth = 2048

    def kernel(x_ref, w_ref, v_ref):
        total = jnp.zeros((rows, cols), F32)
        for start in range(0, width, depth):
            span = slice(start, start + depth)
            total = total + jnp.dot(x_ref[:, span], w_ref[span, :], preferred_element_type=F32)
        v_ref[...] = total.astype(BF16)

    return pl.pallas_call(
        kernel,
        out_shape=jax.ShapeDtypeStruct((rows, cols), BF16),
        in_specs=[VMEM, VMEM],
        out_specs=VMEM,
        compiler_params=grant(14),
        cost_estimate=estimate(2 * rows * width * cols, 2 * width * (cols + rows)),
        name="project",
    )(layer_rows, value_weight)


def masked(block, valid):
    return jnp.where(valid, block, jnp.zeros_like(block))


def lanes(start, size):
    return pl.ds(pl.multiple_of(start, size), size)


def stack_heads(group, heads, source, target, keep):
    rows = source.shape[0]
    for h in range(heads):
        block = source[:, lanes((group * heads + h) * HD, HD)]
        target[h * rows : (h + 1) * rows, :] = keep(block)


def weigh(place, queries, out_grads, keys):
    rows, width = queries.shape
    parts = len(keys)
    kv_width = keys[0].shape[1]
    groups = kv_width // HD
    heads = width // HD // groups
    total = rows * parts
    factor = HD ** (-0.5) * LOG2E
    pair = 2

    def kernel(place_ref, q_ref, o_ref, *rest):
        k_refs, p_ref = rest[:parts], rest[parts]
        v_refs, (q_buf, o_buf) = rest[parts + 1 : 2 * parts + 1], rest[2 * parts + 1 :]
        me, length = place_ref[0], place_ref[1]
        valid = me * rows + lax.broadcasted_iota(jnp.int32, (rows, HD), 0) < length
        row = lax.broadcasted_iota(jnp.int32, (rows, pair * rows), 0)
        lane = lax.broadcasted_iota(jnp.int32, (rows, pair * rows), 1)
        causal = row <= lax.rem(lane, rows)

        @pl.loop(0, groups)
        def _(group):
            cols = lanes(group * HD, HD)
            stack_heads(group, heads, q_ref, q_buf, lambda block: block)
            stack_heads(group, heads, o_ref, o_buf, lambda block: masked(block, valid))
            for h in range(0, heads, pair):
                span = slice(h * rows, (h + pair) * rows)
                q = q_buf[span, :]
                scores = [lax.dot_general(r[:, cols], q, NT, preferred_element_type=F32) for r in k_refs]
                scores[0] = jnp.where(causal, scores[0], -jnp.inf)
                peak = jnp.max(scores[0], axis=0, keepdims=True)
                for k in range(1, parts):
                    higher = jnp.maximum(peak, jnp.max(scores[k], axis=0, keepdims=True))
                    peak = jnp.where((me ^ k) < me, higher, peak)
                peak = peak * factor
                sums = 0.0
                for k in range(parts):
                    shift = peak if k == 0 else jnp.where((me ^ k) < me, peak, jnp.inf)
                    scores[k] = jnp.exp2(scores[k] * factor - shift)
                    sums = sums + jnp.sum(scores[k], axis=0, keepdims=True)
                inverse = 1.0 / sums
                for k in range(parts):
                    p_ref[group, k * rows : (k + 1) * rows, span] = (scores[k] * inverse).astype(BF16)
            for k in range(parts):
                block = p_ref[group, k * rows : (k + 1) * rows, :]
                part = jnp.dot(block, o_buf[...], preferred_element_type=F32)
                v_refs[k][:, cols] = part.astype(v_refs[k].dtype)

    kinds = [F32] + [BF16] * (parts - 1)
    out = pl.pallas_call(
        kernel,
        out_shape=[jax.ShapeDtypeStruct((groups, total, heads * rows), BF16)]
        + [jax.ShapeDtypeStruct((rows, kv_width), kind) for kind in kinds],
        in_specs=[SMEM] + [VMEM] * (2 + parts),
        out_specs=[VMEM] * (1 + parts),
        scratch_shapes=[pltpu.VMEM((heads * rows, HD), BF16)] * 2,
        compiler_params=grant(8 + 2 * parts),
        cost_estimate=estimate(
            HEAVY * 4 * rows * total * width,
            2 * (2 * rows * width + 2 * total * kv_width),
            rows * total * width // HD,
        ),
        name="weigh",
    )(place, queries, out_grads, *keys)
    return out[0], out[1:]


def key_side(place, weights, queries, out_grads, values):
    rows, width = queries.shape
    parts = len(values)
    kv_width = values[0].shape[1]
    groups = kv_width // HD
    heads = width // HD // groups
    total = rows * parts
    scale = HD ** (-0.5)
    pair = 2

    def kernel(place_ref, p_ref, q_ref, o_ref, *rest):
        v_refs, k_refs = rest[:parts], rest[parts : 2 * parts]
        q_buf, o_buf, s_buf = rest[2 * parts :]
        me, length = place_ref[0], place_ref[1]
        valid = me * rows + lax.broadcasted_iota(jnp.int32, (rows, HD), 0) < length

        @pl.loop(0, groups)
        def _(group):
            cols = lanes(group * HD, HD)
            stack_heads(group, heads, q_ref, q_buf, lambda block: block)
            stack_heads(group, heads, o_ref, o_buf, lambda block: masked(block, valid))
            for h in range(0, heads, pair):
                span = slice(h * rows, (h + pair) * rows)
                o = o_buf[span, :]
                grads, offset = [], 0.0
                for k in range(parts):
                    grad = lax.dot_general(v_refs[k][:, cols], o, NT, preferred_element_type=F32)
                    weight = p_ref[group, k * rows : (k + 1) * rows, span].astype(F32)
                    offset = offset + jnp.sum(weight * grad, axis=0, keepdims=True)
                    grads.append(grad)
                for k in range(parts):
                    weight = p_ref[group, k * rows : (k + 1) * rows, span].astype(F32)
                    s_buf[k * rows : (k + 1) * rows, span] = (weight * (grads[k] - offset)).astype(BF16)
            for k in range(parts):
                part = jnp.dot(s_buf[k * rows : (k + 1) * rows, :], q_buf[...], preferred_element_type=F32)
                k_refs[k][:, cols] = (part * scale).astype(k_refs[k].dtype)

    kinds = [F32] + [BF16] * (parts - 1)
    return pl.pallas_call(
        kernel,
        out_shape=[jax.ShapeDtypeStruct((rows, kv_width), kind) for kind in kinds],
        in_specs=[SMEM] + [VMEM] * (3 + parts),
        out_specs=[VMEM] * parts,
        scratch_shapes=[pltpu.VMEM((heads * rows, HD), BF16)] * 2
        + [pltpu.VMEM((total, heads * rows), BF16)],
        compiler_params=grant(8 + 3 * parts),
        cost_estimate=estimate(4 * rows * total * width, 2 * (2 * rows * width + 2 * total * kv_width)),
        name="key_side",
    )(place, weights, queries, out_grads, *values)


def settle(parts_list):
    rows, cols = parts_list[0].shape

    def kernel(*refs):
        total = refs[0][...].astype(F32)
        for r in refs[1:-1]:
            total = total + r[...].astype(F32)
        refs[-1][...] = total.T.astype(BF16)

    return pl.pallas_call(
        kernel,
        out_shape=jax.ShapeDtypeStruct((cols, rows), BF16),
        in_specs=[VMEM] * len(parts_list),
        out_specs=VMEM,
        compiler_params=grant(8),
        cost_estimate=estimate(rows * cols * 4, 10 * rows * cols),
        name="settle",
    )(*parts_list)


def doc_grad(place, value_grads, features, before, blocks):
    parts = len(features)
    rows, chunk = features[0].shape
    cols = value_grads[0].shape[0]
    width = cols // blocks
    half = blocks // 2

    def kernel(place_ref, *refs):
        x_refs, d_refs = refs[:parts], refs[parts : 2 * parts]
        keep_ref, send_ref, square_ref = refs[-3:]
        odd = place_ref[2]
        x = jnp.concatenate([r[...] for r in x_refs], axis=0)

        def side(which):
            picked = []
            for z in range(half):
                block = pl.ds(pl.multiple_of((2 * z + which) * width, width), width)
                picked.append(jnp.concatenate([r[block, :] for r in d_refs], axis=1))
            return jnp.dot(jnp.concatenate(picked, axis=0), x, preferred_element_type=F32)

        kept = side(odd)
        sent = side(1 - odd)
        keep_ref[...] = kept
        send_ref[...] = sent.astype(BF16)
        both = kept * kept + sent * sent
        folded = jnp.sum(both.reshape(half * width // 8, 8, chunk), axis=0)
        squares = sum(folded[:, i * HD : (i + 1) * HD] for i in range(chunk // HD))
        square_ref[...] = squares + (refs[2 * parts][...] if before else 0.0)

    return pl.pallas_call(
        kernel,
        out_shape=[
            jax.ShapeDtypeStruct((half * width, chunk), F32),
            jax.ShapeDtypeStruct((half * width, chunk), BF16),
            jax.ShapeDtypeStruct((8, HD), F32),
        ],
        in_specs=[SMEM] + [VMEM] * (2 * parts + len(before)),
        out_specs=[VMEM] * 3,
        compiler_params=grant(8),
        cost_estimate=estimate(2 * rows * parts * chunk * cols, 2 * rows * parts * (chunk + cols) + 3 * cols * chunk),
        name="doc_grad",
    )(place, *features, *value_grads, *before)


def combine(place, squares, kept, received, order, blocks, clip):
    half = blocks // 2
    tall = kept[0].shape[0]
    sizes = [k.shape[1] for k in kept]
    whole = sum(sizes)
    width = tall // half
    chunks = len(kept)
    count = len(squares)

    def kernel(place_ref, *refs):
        square_refs = refs[:count]
        keep_refs = refs[count : count + chunks]
        got_refs = refs[count + chunks : count + 2 * chunks]
        norm_ref, outs = refs[count + 2 * chunks], refs[count + 2 * chunks + 1 :]
        sums = square_refs[0][...]
        for r in square_refs[1:]:
            sums = sums + r[...]

        def norm(block):
            lanes = jnp.sum(block, axis=1, keepdims=True)
            return jnp.sqrt(jnp.sum(lanes, axis=0, keepdims=True))

        mine, other = norm(sums[:8]), norm(sums[8:])
        norm_ref[...] = jnp.broadcast_to(mine, (8, HD))
        mine, other = clip / (mine + 0.01), clip / (other + 0.01)
        for i in range(half):
            rows = pl.ds(pl.multiple_of(place_ref[order + i] * width, width), width)
            for j in range(chunks):
                total = keep_refs[j][rows, :] * mine + got_refs[j][rows, :].astype(F32) * other
                start = sum(sizes[:j])
                outs[i][:, start : start + sizes[j]] = total.astype(BF16)

    out = pl.pallas_call(
        kernel,
        out_shape=[jax.ShapeDtypeStruct((8, HD), F32)]
        + [jax.ShapeDtypeStruct((width, whole), BF16)] * half,
        in_specs=[SMEM] + [VMEM] * (count + 2 * chunks),
        out_specs=[VMEM] * (half + 1),
        compiler_params=grant(12),
        cost_estimate=estimate(4 * tall * whole, 8 * tall * whole),
        name="combine",
    )(place, *squares, *kept, *received)
    return out[0], out[1:]


def relay(place, flag, mine, got):
    def kernel(place_ref, mine_ref, got_ref, out_ref):
        got = got_ref[...].astype(F32)
        got = jnp.where(place_ref[flag] == 1, got, jnp.zeros_like(got))
        out_ref[...] = (mine_ref[...].astype(F32) + got).astype(BF16)

    return pl.pallas_call(
        kernel,
        out_shape=jax.ShapeDtypeStruct(mine.shape, BF16),
        in_specs=[SMEM, VMEM, VMEM],
        out_specs=VMEM,
        compiler_params=grant(8),
        cost_estimate=estimate(2 * mine.size, 6 * mine.size),
        name="relay",
    )(place, mine, got)


def add_up(place, flag, gated, terms, kind):
    def kernel(place_ref, *refs):
        total = refs[len(gated)][...].astype(F32)
        for r in refs[len(gated) + 1 : -1]:
            total = total + r[...].astype(F32)
        for r in refs[: len(gated)]:
            got = r[...].astype(F32)
            total = total + jnp.where(place_ref[flag] == 1, jnp.zeros_like(got), got)
        refs[-1][...] = total.astype(kind)

    size = terms[0].size
    return pl.pallas_call(
        kernel,
        out_shape=jax.ShapeDtypeStruct(terms[0].shape, kind),
        in_specs=[SMEM] + [VMEM] * (len(gated) + len(terms)),
        out_specs=VMEM,
        compiler_params=grant(8),
        cost_estimate=estimate(8 * size, 14 * size),
        name="add_up",
    )(place, *gated, *terms)


def step(layer_input, value_weight, queries, key_states, out_grads, lengths):
    parts = lax.axis_size("context")
    docs = lax.axis_size("dp")
    planes = docs // 2
    context = lax.axis_index("context")
    doc = lax.axis_index("dp")
    z = doc // 2
    if planes == 4:
        order = [z, 3 * (1 - z % 2), 2 - z // 2]
        order.append(6 - sum(order))
    else:
        order = [z ^ k for k in range(planes)]
    inner = (z > 0) & (z < planes - 1)
    place = jnp.stack([context, lengths[0], doc % 2, z, inner] + order).astype(jnp.int32)
    width = layer_input.shape[2]
    sizes = split(width // parts)
    cols = value_weight.shape[1]

    def over_context(x, k):
        return lax.ppermute(x, "context", [(i, i ^ k) for i in range(parts)])

    def over_planes(x, hops):
        return lax.ppermute(x, "dp", [(2 * a + c, 2 * b + c) for a, b in hops for c in range(2)])

    def over_cores(x):
        return lax.ppermute(x, "dp", [(i, i ^ 1) for i in range(docs)])

    keys = [key_states[0]] + [over_context(key_states[0], k) for k in range(1, parts)]
    pieces = cut(place, layer_input[0], parts, sizes)
    features = []
    for j in range(len(sizes)):
        features.append([pieces[0][j]] + [over_context(pieces[k][j], k) for k in range(1, parts)])
    weights, value_parts = weigh(place, queries[0], out_grads[0], keys)
    blocks = [value_parts[0]] + [over_context(value_parts[k], k) for k in range(1, parts)]
    value_low = settle(blocks)
    value_grads = [value_low] + [over_context(value_low, k) for k in range(1, parts)]

    kept, received, square = [], [], []
    for j in range(len(sizes)):
        keep, send, *square = doc_grad(place, value_grads, features[j], square, docs)
        kept.append(keep)
        received.append(over_cores(send))
    squares = jnp.concatenate([square[0], over_cores(square[0])], axis=0)
    squares = [squares] + [over_context(squares, k) for k in range(1, parts)]
    norm, shares = combine(place, squares, kept, received, 5, docs, math.sqrt(width * cols))

    own_values = project(layer_input[0], value_weight)
    values = [own_values] + [over_context(own_values, k) for k in range(1, parts)]
    key_parts = key_side(place, weights, queries[0], out_grads[0], values)
    key_blocks = [key_parts[0]] + [over_context(key_parts[k], k) for k in range(1, parts)]
    key_grads = add_up(place, 4, [], key_blocks, BF16)[None]

    if planes == 4:
        first = over_planes(shares[1], [(0, 1), (1, 0), (2, 3), (3, 2)])
        far = over_planes(shares[2], [(0, 2), (3, 1)])
        near = over_planes(shares[2], [(1, 2), (2, 1)])
        onward = relay(place, 4, shares[3], first)
        last = over_planes(onward, [(0, 1), (3, 2), (1, 3), (2, 0)])
        total = add_up(place, 4, [first], [shares[0], far, near, last], F32)
    else:
        got = [over_planes(shares[k], [(i, i ^ k) for i in range(planes)]) for k in range(1, planes)]
        total = add_up(place, 4, [], [shares[0]] + got, F32)
    return total.T, norm[0, :1], key_grads


def solution(mesh):
    placed = (
        P("dp", "context", None),
        P(),
        P("dp", "context", None),
        P("dp", "context", None),
        P("dp", "context", None),
        P("dp"),
    )
    return jax.shard_map(
        step,
        mesh=mesh,
        in_specs=placed,
        out_specs=(P("context", "dp"), P("dp"), P("dp", "context", None)),
        check_vma=False,
    )
```

```python
import math

import jax
import jax.numpy as jnp
from jax import lax
from jax.experimental import pallas as pl
from jax.experimental.pallas import tpu as pltpu
from jax.sharding import PartitionSpec as P

HD = 128
LANES = 128
TERMS = 8
EARLY_SHARE = 6
FIRST_SHARE = 8
HEAVY = 10
F32 = jnp.float32
BF16 = jnp.bfloat16
LOG2E = 1.4426950408889634


NT = (((1,), (1,)), ((), ()))
VMEM = pl.BlockSpec(memory_space=pltpu.VMEM)
SMEM = pl.BlockSpec(memory_space=pltpu.SMEM)


def estimate(flops, nbytes, exps=0):
    return pl.CostEstimate(flops=flops, bytes_accessed=nbytes, transcendentals=exps)


def grant(mib):
    return pltpu.CompilerParams(vmem_limit_bytes=mib << 20)


def split(own):
    units = own // LANES
    first = max(1, units * FIRST_SHARE // 16)
    return [first * LANES, (units - first) * LANES]


def cut(place, layer_rows, parts, sizes):
    rows, width = layer_rows.shape
    own = width // parts
    chunks = len(sizes)

    def kernel(place_ref, x_ref, *outs):
        for k in range(parts):
            start = (place_ref[0] ^ k) * own
            for j in range(chunks):
                span = pl.ds(pl.multiple_of(start + sum(sizes[:j]), LANES), sizes[j])
                outs[k * chunks + j][...] = x_ref[:, span]

    out = pl.pallas_call(
        kernel,
        out_shape=[jax.ShapeDtypeStruct((rows, size), BF16) for _ in range(parts) for size in sizes],
        in_specs=[SMEM, VMEM],
        out_specs=[VMEM] * (parts * chunks),
        compiler_params=grant(8),
        cost_estimate=estimate(0, HEAVY * 4 * rows * width),
        name="cut",
    )(place, layer_rows)
    return [[out[k * chunks + j] for j in range(chunks)] for k in range(parts)]


def anchor():
    def kernel(out_ref):
        out_ref[...] = jnp.zeros((8, HD), F32)

    return pl.pallas_call(
        kernel,
        out_shape=jax.ShapeDtypeStruct((8, HD), F32),
        out_specs=VMEM,
        compiler_params=grant(1),
        cost_estimate=estimate(10**10, 0),
        name="anchor",
    )()


def project(layer_rows, value_weight):
    rows, width = layer_rows.shape
    cols = value_weight.shape[1]
    depth = 2048

    def kernel(x_ref, w_ref, v_ref):
        total = jnp.zeros((rows, cols), F32)
        for start in range(0, width, depth):
            span = slice(start, start + depth)
            total = total + jnp.dot(x_ref[:, span], w_ref[span, :], preferred_element_type=F32)
        v_ref[...] = total.astype(BF16)

    return pl.pallas_call(
        kernel,
        out_shape=jax.ShapeDtypeStruct((rows, cols), BF16),
        in_specs=[VMEM, VMEM],
        out_specs=VMEM,
        compiler_params=grant(14),
        cost_estimate=estimate(2 * rows * width * cols, 2 * width * (cols + rows)),
        name="project",
    )(layer_rows, value_weight)


def masked(block, valid):
    return jnp.where(valid, block, jnp.zeros_like(block))


def lanes(start, size):
    return pl.ds(pl.multiple_of(start, size), size)


def stack_heads(group, heads, source, target, keep):
    rows = source.shape[0]
    for h in range(heads):
        block = source[:, lanes((group * heads + h) * HD, HD)]
        target[h * rows : (h + 1) * rows, :] = keep(block)


def weigh(place, queries, out_grads, keys):
    rows, width = queries.shape
    parts = len(keys)
    kv_width = keys[0].shape[1]
    groups = kv_width // HD
    heads = width // HD // groups
    total = rows * parts
    factor = HD ** (-0.5) * LOG2E
    pair = 2

    def kernel(place_ref, q_ref, o_ref, *rest):
        k_refs, p_ref = rest[:parts], rest[parts]
        v_refs, (q_buf, o_buf) = rest[parts + 1 : 2 * parts + 1], rest[2 * parts + 1 :]
        me, length = place_ref[0], place_ref[1]
        valid = me * rows + lax.broadcasted_iota(jnp.int32, (rows, HD), 0) < length
        row = lax.broadcasted_iota(jnp.int32, (rows, pair * rows), 0)
        lane = lax.broadcasted_iota(jnp.int32, (rows, pair * rows), 1)
        causal = row <= lax.rem(lane, rows)

        @pl.loop(0, groups)
        def _(group):
            cols = lanes(group * HD, HD)
            stack_heads(group, heads, q_ref, q_buf, lambda block: block)
            stack_heads(group, heads, o_ref, o_buf, lambda block: masked(block, valid))
            for h in range(0, heads, pair):
                span = slice(h * rows, (h + pair) * rows)
                q = q_buf[span, :]
                scores = [lax.dot_general(r[:, cols], q, NT, preferred_element_type=F32) for r in k_refs]
                scores[0] = jnp.where(causal, scores[0], -jnp.inf)
                peak = jnp.max(scores[0], axis=0, keepdims=True)
                for k in range(1, parts):
                    higher = jnp.maximum(peak, jnp.max(scores[k], axis=0, keepdims=True))
                    peak = jnp.where((me ^ k) < me, higher, peak)
                peak = peak * factor
                sums = 0.0
                for k in range(parts):
                    shift = peak if k == 0 else jnp.where((me ^ k) < me, peak, jnp.inf)
                    scores[k] = jnp.exp2(scores[k] * factor - shift)
                    sums = sums + jnp.sum(scores[k], axis=0, keepdims=True)
                inverse = 1.0 / sums
                for k in range(parts):
                    p_ref[group, k * rows : (k + 1) * rows, span] = (scores[k] * inverse).astype(BF16)
            for k in range(parts):
                block = p_ref[group, k * rows : (k + 1) * rows, :]
                part = jnp.dot(block, o_buf[...], preferred_element_type=F32)
                v_refs[k][:, cols] = part.astype(v_refs[k].dtype)

    kinds = [F32] + [BF16] * (parts - 1)
    out = pl.pallas_call(
        kernel,
        out_shape=[jax.ShapeDtypeStruct((groups, total, heads * rows), BF16)]
        + [jax.ShapeDtypeStruct((rows, kv_width), kind) for kind in kinds],
        in_specs=[SMEM] + [VMEM] * (2 + parts),
        out_specs=[VMEM] * (1 + parts),
        scratch_shapes=[pltpu.VMEM((heads * rows, HD), BF16)] * 2,
        compiler_params=grant(8 + 2 * parts),
        cost_estimate=estimate(
            HEAVY * 4 * rows * total * width,
            2 * (2 * rows * width + 2 * total * kv_width),
            rows * total * width // HD,
        ),
        name="weigh",
    )(place, queries, out_grads, *keys)
    return out[0], out[1:]


def key_side(place, weights, queries, out_grads, values):
    rows, width = queries.shape
    parts = len(values)
    kv_width = values[0].shape[1]
    groups = kv_width // HD
    heads = width // HD // groups
    total = rows * parts
    scale = HD ** (-0.5)
    pair = 2

    def kernel(place_ref, p_ref, q_ref, o_ref, *rest):
        v_refs, k_refs = rest[:parts], rest[parts : 2 * parts]
        q_buf, o_buf, s_buf = rest[2 * parts :]
        me, length = place_ref[0], place_ref[1]
        valid = me * rows + lax.broadcasted_iota(jnp.int32, (rows, HD), 0) < length

        @pl.loop(0, groups)
        def _(group):
            cols = lanes(group * HD, HD)
            stack_heads(group, heads, q_ref, q_buf, lambda block: block)
            stack_heads(group, heads, o_ref, o_buf, lambda block: masked(block, valid))
            for h in range(0, heads, pair):
                span = slice(h * rows, (h + pair) * rows)
                o = o_buf[span, :]
                grads, offset = [], 0.0
                for k in range(parts):
                    grad = lax.dot_general(v_refs[k][:, cols], o, NT, preferred_element_type=F32)
                    weight = p_ref[group, k * rows : (k + 1) * rows, span].astype(F32)
                    offset = offset + jnp.sum(weight * grad, axis=0, keepdims=True)
                    grads.append(grad)
                for k in range(parts):
                    weight = p_ref[group, k * rows : (k + 1) * rows, span].astype(F32)
                    s_buf[k * rows : (k + 1) * rows, span] = (weight * (grads[k] - offset)).astype(BF16)
            for k in range(parts):
                part = jnp.dot(s_buf[k * rows : (k + 1) * rows, :], q_buf[...], preferred_element_type=F32)
                k_refs[k][:, cols] = (part * scale).astype(k_refs[k].dtype)

    kinds = [F32] + [BF16] * (parts - 1)
    return pl.pallas_call(
        kernel,
        out_shape=[jax.ShapeDtypeStruct((rows, kv_width), kind) for kind in kinds],
        in_specs=[SMEM] + [VMEM] * (3 + parts),
        out_specs=[VMEM] * parts,
        scratch_shapes=[pltpu.VMEM((heads * rows, HD), BF16)] * 2
        + [pltpu.VMEM((total, heads * rows), BF16)],
        compiler_params=grant(8 + 3 * parts),
        cost_estimate=estimate(4 * rows * total * width, 2 * (2 * rows * width + 2 * total * kv_width)),
        name="key_side",
    )(place, weights, queries, out_grads, *values)


def settle(parts_list):
    rows, cols = parts_list[0].shape

    def kernel(*refs):
        total = refs[0][...].astype(F32)
        for r in refs[1:-1]:
            total = total + r[...].astype(F32)
        refs[-1][...] = total.T.astype(BF16)

    return pl.pallas_call(
        kernel,
        out_shape=jax.ShapeDtypeStruct((cols, rows), BF16),
        in_specs=[VMEM] * len(parts_list),
        out_specs=VMEM,
        compiler_params=grant(8),
        cost_estimate=estimate(rows * cols * 4, 10 * rows * cols),
        name="settle",
    )(*parts_list)


def doc_grad(place, value_grads, features, spans, before, blocks, kind):
    parts = len(value_grads)
    rows = features[0][0].shape[0]
    chunk = sum(size for _, size in spans)
    cols = value_grads[0].shape[0]
    width = cols // blocks
    half = blocks // 2
    count = parts * len(spans)

    def kernel(place_ref, *refs):
        x_refs, d_refs = refs[:count], refs[count : count + parts]
        keep_ref, send_ref, square_ref = refs[-3:]
        odd = place_ref[2]

        def picked(which):
            blocks_of = []
            for z in range(half):
                block = pl.ds(pl.multiple_of((2 * z + which) * width, width), width)
                blocks_of.append(jnp.concatenate([r[block, :] for r in d_refs], axis=1))
            return jnp.concatenate(blocks_of, axis=0)

        ours, theirs = picked(odd), picked(1 - odd)
        squares = refs[count + parts][...]
        at = 0
        for i, (start, size) in enumerate(spans):
            span = slice(start, start + size)
            x = jnp.concatenate([r[:, span] for r in x_refs[i * parts : (i + 1) * parts]], axis=0)
            kept = jnp.dot(ours, x, preferred_element_type=F32)
            sent = jnp.dot(theirs, x, preferred_element_type=F32)
            keep_ref[:, at : at + size] = kept.astype(kind)
            send_ref[:, at : at + size] = sent.astype(BF16)
            both = kept * kept + sent * sent
            folded = jnp.sum(both.reshape(half * width // 8, 8, size), axis=0)
            for j in range(size // HD):
                squares = squares + folded[:, j * HD : (j + 1) * HD]
            at += size
        square_ref[...] = squares

    inputs = [x for chunk_of in features for x in chunk_of]
    return pl.pallas_call(
        kernel,
        out_shape=[
            jax.ShapeDtypeStruct((half * width, chunk), kind),
            jax.ShapeDtypeStruct((half * width, chunk), BF16),
            jax.ShapeDtypeStruct((8, HD), F32),
        ],
        in_specs=[SMEM] + [VMEM] * (count + parts + 1),
        out_specs=[VMEM] * 3,
        compiler_params=grant(10),
        cost_estimate=estimate(2 * rows * parts * chunk * cols, 2 * rows * parts * (chunk + cols) + 3 * cols * chunk),
        name="doc_grad",
    )(place, *inputs, *value_grads, before)


def pack(place, kept, received, blocks):
    half = blocks // 2
    tall, chunk = kept.shape
    width = tall // half

    def kernel(place_ref, keep_ref, got_ref, *outs):
        for k in range(half):
            rows = pl.ds(pl.multiple_of((place_ref[3] ^ k) * width, width), width)
            outs[k][:width, :] = keep_ref[rows, :]
            outs[k][width:, :] = got_ref[rows, :]

    return pl.pallas_call(
        kernel,
        out_shape=[jax.ShapeDtypeStruct((2 * width, chunk), BF16)] * half,
        in_specs=[SMEM, VMEM, VMEM],
        out_specs=[VMEM] * half,
        compiler_params=grant(8),
        cost_estimate=estimate(0, 8 * tall * chunk),
        name="pack",
    )(place, kept, received)


def finish(place, flag, own, plain, mine, first, others):
    planes = len(plain)
    width = plain[0].shape[0] // 2
    chunk = plain[0].shape[1]
    rest = mine.shape[1] - LANES

    def kernel(place_ref, own_ref, *refs):
        plain_refs, (mine_ref, *got_refs, out_ref) = refs[:planes], refs[planes:]
        factors = [[own_ref[:1, :1], own_ref[8:9, :1]]]
        sums = mine_ref[:, :rest].astype(F32)
        if flag is None:
            for r in got_refs:
                factors.append(gather_terms(r[:TERMS, rest:]))
                sums = sums + r[:, :rest].astype(F32)
        else:
            first_ref, far_ref, near_ref, last_ref = got_refs
            inner = place_ref[flag] == 1
            factors.append(gather_terms(first_ref[:TERMS, rest:]))
            last = last_ref[: 2 * TERMS, rest:]
            for ref, start in ((far_ref, 0), (near_ref, TERMS)):
                direct = gather_terms(ref[:TERMS, rest:])
                passed = gather_terms(last[start : start + TERMS])
                factors.append([jnp.where(inner, d, p) for d, p in zip(direct, passed)])
            for r in got_refs[1:]:
                sums = sums + r[:, :rest].astype(F32)
            got = first_ref[:, :rest].astype(F32)
            sums = sums + jnp.where(inner, jnp.zeros_like(got), got)
        out_ref[:, chunk:] = sums
        total = 0.0
        for (even, odd), r in zip(factors, plain_refs):
            total = total + r[:width, :].astype(F32) * even + r[width:, :].astype(F32) * odd
        out_ref[:, :chunk] = total

    args = [own, *plain, mine, first, *others]
    return pl.pallas_call(
        kernel,
        out_shape=jax.ShapeDtypeStruct((width, chunk + rest), F32),
        in_specs=[SMEM] + [VMEM] * len(args),
        out_specs=VMEM,
        compiler_params=grant(8),
        cost_estimate=estimate(12 * width * (chunk + rest), 20 * width * (chunk + rest)),
        name="finish",
    )(place, *args)


def spread(value):
    rest = jnp.broadcast_to(value, (1, LANES))
    terms = []
    for _ in range(3):
        term = rest.astype(BF16)
        rest = rest - term.astype(F32)
        terms.append(term)
    return terms + [jnp.zeros((1, LANES), BF16)]


def gather_terms(block):
    block = block.astype(F32)
    return [block[i : i + 1, :1] + block[i + 1 : i + 2, :1] + block[i + 2 : i + 3, :1] for i in (0, 4)]


def combine(place, squares, kept, received, order, blocks, clip):
    half = blocks // 2
    tall = kept[0].shape[0]
    sizes = [k.shape[1] for k in kept]
    whole = sum(sizes)
    width = tall // half
    chunks = len(kept)
    count = len(squares)

    def kernel(place_ref, *refs):
        square_refs = refs[:count]
        keep_refs = refs[count : count + chunks]
        got_refs = refs[count + chunks : count + 2 * chunks]
        norm_ref, factor_ref = refs[count + 2 * chunks : count + 2 * chunks + 2]
        outs = refs[count + 2 * chunks + 2 :]
        sums = square_refs[0][...]
        for r in square_refs[1:]:
            sums = sums + r[...]

        def norm(block):
            lanes = jnp.sum(block, axis=1, keepdims=True)
            return jnp.sqrt(jnp.sum(lanes, axis=0, keepdims=True))

        mine, other = norm(sums[:8]), norm(sums[8:])
        norm_ref[...] = jnp.broadcast_to(mine, (8, HD))
        mine, other = clip / (mine + 0.01), clip / (other + 0.01)
        factor_ref[:8, :] = jnp.broadcast_to(mine, (8, HD))
        factor_ref[8:, :] = jnp.broadcast_to(other, (8, HD))
        terms = jnp.concatenate(spread(mine) + spread(other), axis=0)
        for i in range(half):
            outs[i][:TERMS, whole:] = terms
            outs[i][TERMS:, whole:] = jnp.zeros((width - TERMS, LANES), BF16)
            rows = pl.ds(pl.multiple_of(place_ref[order + i] * width, width), width)
            for j in range(chunks):
                total = keep_refs[j][rows, :] * mine + got_refs[j][rows, :].astype(F32) * other
                start = sum(sizes[:j])
                outs[i][:, start : start + sizes[j]] = total.astype(BF16)

    out = pl.pallas_call(
        kernel,
        out_shape=[jax.ShapeDtypeStruct((8, HD), F32), jax.ShapeDtypeStruct((16, HD), F32)]
        + [jax.ShapeDtypeStruct((width, whole + LANES), BF16)] * half,
        in_specs=[SMEM] + [VMEM] * (count + 2 * chunks),
        out_specs=[VMEM] * (half + 2),
        compiler_params=grant(12),
        cost_estimate=estimate(4 * tall * whole, 8 * tall * whole),
        name="combine",
    )(place, *squares, *kept, *received)
    return out[0], out[1], out[2:]


def relay(place, flag, mine, got):
    whole = mine.shape[1] - LANES

    def kernel(place_ref, mine_ref, got_ref, out_ref):
        got = got_ref[:, :whole].astype(F32)
        got = jnp.where(place_ref[flag] == 1, got, jnp.zeros_like(got))
        out_ref[:, :whole] = (mine_ref[:, :whole].astype(F32) + got).astype(BF16)
        out_ref[:, whole:] = mine_ref[:, whole:]
        out_ref[TERMS : 2 * TERMS, whole:] = got_ref[:TERMS, whole:]

    return pl.pallas_call(
        kernel,
        out_shape=jax.ShapeDtypeStruct(mine.shape, BF16),
        in_specs=[SMEM, VMEM, VMEM],
        out_specs=VMEM,
        compiler_params=grant(8),
        cost_estimate=estimate(2 * mine.size, 6 * mine.size),
        name="relay",
    )(place, mine, got)


def add_up(place, flag, gated, terms, kind):
    def kernel(place_ref, *refs):
        total = refs[len(gated)][...].astype(F32)
        for r in refs[len(gated) + 1 : -1]:
            total = total + r[...].astype(F32)
        for r in refs[: len(gated)]:
            got = r[...].astype(F32)
            total = total + jnp.where(place_ref[flag] == 1, jnp.zeros_like(got), got)
        refs[-1][...] = total.astype(kind)

    size = terms[0].size
    return pl.pallas_call(
        kernel,
        out_shape=jax.ShapeDtypeStruct(terms[0].shape, kind),
        in_specs=[SMEM] + [VMEM] * (len(gated) + len(terms)),
        out_specs=VMEM,
        compiler_params=grant(8),
        cost_estimate=estimate(8 * size, 14 * size),
        name="add_up",
    )(place, *gated, *terms)


def step(layer_input, value_weight, queries, key_states, out_grads, lengths):
    parts = lax.axis_size("context")
    docs = lax.axis_size("dp")
    planes = docs // 2
    context = lax.axis_index("context")
    doc = lax.axis_index("dp")
    z = doc // 2
    if planes == 4:
        order = [z, 3 * (1 - z % 2), 2 - z // 2]
        order.append(6 - sum(order))
    else:
        order = [z ^ k for k in range(planes)]
    inner = (z > 0) & (z < planes - 1)
    place = jnp.stack([context, lengths[0], doc % 2, z, inner] + order).astype(jnp.int32)
    width = layer_input.shape[2]
    sizes = split(width // parts)
    early = max(1, width // parts // LANES * EARLY_SHARE // 16) * LANES
    spans = [(early, sizes[0] - early), (0, sizes[1])]
    start = 0 if early < sizes[0] else 1
    spans = spans[start:]
    cols = value_weight.shape[1]

    def over_context(x, k):
        return lax.ppermute(x, "context", [(i, i ^ k) for i in range(parts)])

    def to_later(x, k):
        return lax.ppermute(x, "context", [(i, i ^ k) for i in range(parts) ])

    def to_earlier(x, k):
        return lax.ppermute(x, "context", [(i, i ^ k) for i in range(parts) ])

    def over_planes(x, hops):
        return lax.ppermute(x, "dp", [(2 * a + c, 2 * b + c) for a, b in hops for c in range(2)])

    def swap(k):
        return [(i, i ^ k) for i in range(planes)]

    def over_cores(x):
        return lax.ppermute(x, "dp", [(i, i ^ 1) for i in range(docs)])

    zeros = anchor()
    keys = [key_states[0]] + [to_later(key_states[0], k) for k in range(1, parts)]
    pieces = cut(place, layer_input[0], parts, sizes)
    features = []
    for j in range(len(sizes)):
        features.append([pieces[0][j]] + [over_context(pieces[k][j], k) for k in range(1, parts)])
    weights, value_parts = weigh(place, queries[0], out_grads[0], keys)
    blocks = [value_parts[0]] + [to_earlier(value_parts[k], k) for k in range(1, parts)]
    value_low = settle(blocks)
    value_grads = [value_low] + [over_context(value_low, k) for k in range(1, parts)]

    keep, send, square = doc_grad(place, value_grads, features[:1], [(0, early)], zeros, docs, BF16)
    got = over_cores(send)
    plain = pack(place, keep, got, docs)
    plain = [plain[0]] + [over_planes(plain[k], swap(k)) for k in range(1, planes)]
    keep, send, square = doc_grad(place, value_grads, features[start:], spans, square, docs, F32)
    got = over_cores(send)
    squares = jnp.concatenate([square, over_cores(square)], axis=0)
    squares = [squares] + [over_context(squares, k) for k in range(1, parts)]
    norm, factors, shares = combine(place, squares, [keep], [got], 5, docs, math.sqrt(width * cols))


    own_values = project(layer_input[0], value_weight)
    values = [own_values] + [to_later(own_values, k) for k in range(1, parts)]
    key_parts = key_side(place, weights, queries[0], out_grads[0], values)
    key_blocks = [key_parts[0]] + [to_earlier(key_parts[k], k) for k in range(1, parts)]
    key_grads = add_up(place, 4, [], key_blocks, BF16)[None]

    if planes == 4:
        first = over_planes(shares[1], [(0, 1), (1, 0), (2, 3), (3, 2)])
        far = over_planes(shares[2], [(0, 2), (3, 1)])
        near = over_planes(shares[2], [(1, 2), (2, 1)])
        onward = relay(place, 4, shares[3], first)
        last = over_planes(onward, [(0, 1), (3, 2), (1, 3), (2, 0)])
        total = finish(place, 4, factors, plain, shares[0], first, [far, near, last])
    else:
        got = [over_planes(shares[k], swap(k)) for k in range(1, planes)]
        total = finish(place, None, factors, plain, shares[0], got[0], got[1:])
    return total.T, norm[0, :1], key_grads


def solution(mesh):
    placed = (
        P("dp", "context", None),
        P(),
        P("dp", "context", None),
        P("dp", "context", None),
        P("dp", "context", None),
        P("dp"),
    )
    return jax.shard_map(
        step,
        mesh=mesh,
        in_specs=placed,
        out_specs=(P("context", "dp"), P("dp"), P("dp", "context", None)),
        check_vma=False,
    )
```

```python
import math

import jax
import jax.numpy as jnp
from jax import lax
from jax.experimental import pallas as pl
from jax.experimental.pallas import tpu as pltpu
from jax.sharding import PartitionSpec as P

HD = 128
LANES = 128
TERMS = 8
EARLY_SHARE = 6
FIRST_SHARE = 8
HEAVY = 10
F32 = jnp.float32
BF16 = jnp.bfloat16
LOG2E = 1.4426950408889634


NT = (((1,), (1,)), ((), ()))
VMEM = pl.BlockSpec(memory_space=pltpu.VMEM)
SMEM = pl.BlockSpec(memory_space=pltpu.SMEM)


def estimate(flops, nbytes, exps=0):
    return pl.CostEstimate(flops=flops, bytes_accessed=nbytes, transcendentals=exps)


def grant(mib):
    return pltpu.CompilerParams(vmem_limit_bytes=mib << 20)


def split(own):
    units = own // LANES
    first = max(1, units * FIRST_SHARE // 16)
    return [first * LANES, (units - first) * LANES]


def cut(place, layer_rows, out_grads, queries, parts, sizes):
    rows, width = layer_rows.shape
    own = width // parts
    chunks = len(sizes)
    heads = out_grads.shape[1]

    def kernel(place_ref, x_ref, o_ref, q_ref, *refs):
        outs, (grad_ref, query_ref) = refs[: parts * chunks], refs[parts * chunks :]
        for k in range(parts):
            start = (place_ref[0] ^ k) * own
            for j in range(chunks):
                span = pl.ds(pl.multiple_of(start + sum(sizes[:j]), LANES), sizes[j])
                outs[k * chunks + j][...] = x_ref[:, span]
        me, length = place_ref[0], place_ref[1]
        valid = me * rows + lax.broadcasted_iota(jnp.int32, (rows, LANES), 0) < length
        for start in range(0, heads, LANES):
            block = o_ref[:, start : start + LANES]
            grad_ref[:, start : start + LANES] = jnp.where(valid, block, jnp.zeros_like(block))
        query_ref[...] = q_ref[...]

    out = pl.pallas_call(
        kernel,
        out_shape=[jax.ShapeDtypeStruct((rows, size), BF16) for _ in range(parts) for size in sizes]
        + [jax.ShapeDtypeStruct(out_grads.shape, BF16)] * 2,
        in_specs=[SMEM] + [VMEM] * 3,
        out_specs=[VMEM] * (parts * chunks + 2),
        compiler_params=grant(12),
        cost_estimate=estimate(0, HEAVY * 4 * rows * width),
        name="cut",
    )(place, layer_rows, out_grads, queries)
    return [[out[k * chunks + j] for j in range(chunks)] for k in range(parts)], *out[-2:]


def anchor():
    def kernel(out_ref):
        out_ref[...] = jnp.zeros((8, HD), F32)

    return pl.pallas_call(
        kernel,
        out_shape=jax.ShapeDtypeStruct((8, HD), F32),
        out_specs=VMEM,
        compiler_params=grant(1),
        cost_estimate=estimate(10**10, 0),
        name="anchor",
    )()


def project(layer_rows, value_weight):
    rows, width = layer_rows.shape
    cols = value_weight.shape[1]
    depth = 2048

    def kernel(x_ref, w_ref, v_ref):
        total = jnp.zeros((rows, cols), F32)
        for start in range(0, width, depth):
            span = slice(start, start + depth)
            total = total + jnp.dot(x_ref[:, span], w_ref[span, :], preferred_element_type=F32)
        v_ref[...] = total.astype(BF16)

    return pl.pallas_call(
        kernel,
        out_shape=jax.ShapeDtypeStruct((rows, cols), BF16),
        in_specs=[VMEM, VMEM],
        out_specs=VMEM,
        compiler_params=grant(14),
        cost_estimate=estimate(2 * rows * width * cols, 2 * width * (cols + rows)),
        name="project",
    )(layer_rows, value_weight)


def lanes(start, size):
    return pl.ds(pl.multiple_of(start, size), size)


def stack_heads(group, heads, source, target):
    rows = source.shape[0]
    for h in range(heads):
        target[h * rows : (h + 1) * rows, :] = source[:, lanes((group * heads + h) * HD, HD)]


def weigh(place, queries, out_grads, keys):
    rows, width = queries.shape
    parts = len(keys)
    kv_width = keys[0].shape[1]
    groups = kv_width // HD
    heads = width // HD // groups
    total = rows * parts
    factor = HD ** (-0.5) * LOG2E
    pair = 2

    def kernel(place_ref, q_ref, o_ref, *rest):
        k_refs, p_ref = rest[:parts], rest[parts]
        v_refs, (q_buf, o_buf) = rest[parts + 1 : 2 * parts + 1], rest[2 * parts + 1 :]
        me = place_ref[0]
        row = lax.broadcasted_iota(jnp.int32, (rows, pair * rows), 0)
        lane = lax.broadcasted_iota(jnp.int32, (rows, pair * rows), 1)
        causal = row <= lax.rem(lane, rows)

        @pl.loop(0, groups)
        def _(group):
            cols = lanes(group * HD, HD)
            stack_heads(group, heads, q_ref, q_buf)
            stack_heads(group, heads, o_ref, o_buf)
            for h in range(0, heads, pair):
                span = slice(h * rows, (h + pair) * rows)
                q = q_buf[span, :]
                scores = [lax.dot_general(r[:, cols], q, NT, preferred_element_type=F32) for r in k_refs]
                scores[0] = jnp.where(causal, scores[0], -jnp.inf)
                peak = jnp.max(scores[0], axis=0, keepdims=True)
                for k in range(1, parts):
                    higher = jnp.maximum(peak, jnp.max(scores[k], axis=0, keepdims=True))
                    peak = jnp.where((me ^ k) < me, higher, peak)
                peak = peak * factor
                sums = 0.0
                for k in range(parts):
                    shift = peak if k == 0 else jnp.where((me ^ k) < me, peak, jnp.inf)
                    scores[k] = jnp.exp2(scores[k] * factor - shift)
                    sums = sums + jnp.sum(scores[k], axis=0, keepdims=True)
                inverse = 1.0 / sums
                for k in range(parts):
                    p_ref[group, k * rows : (k + 1) * rows, span] = (scores[k] * inverse).astype(BF16)
            for k in range(parts):
                block = p_ref[group, k * rows : (k + 1) * rows, :]
                part = jnp.dot(block, o_buf[...], preferred_element_type=F32)
                v_refs[k][:, cols] = part.astype(v_refs[k].dtype)

    kinds = [F32] + [BF16] * (parts - 1)
    out = pl.pallas_call(
        kernel,
        out_shape=[jax.ShapeDtypeStruct((groups, total, heads * rows), BF16)]
        + [jax.ShapeDtypeStruct((rows, kv_width), kind) for kind in kinds],
        in_specs=[SMEM] + [VMEM] * (2 + parts),
        out_specs=[VMEM] * (1 + parts),
        scratch_shapes=[pltpu.VMEM((heads * rows, HD), BF16)] * 2,
        compiler_params=grant(8 + 2 * parts),
        cost_estimate=estimate(
            HEAVY * 4 * rows * total * width,
            2 * (2 * rows * width + 2 * total * kv_width),
            rows * total * width // HD,
        ),
        name="weigh",
    )(place, queries, out_grads, *keys)
    return out[0], out[1:]


def key_side(weights, queries, out_grads, values):
    rows, width = queries.shape
    parts = len(values)
    kv_width = values[0].shape[1]
    groups = kv_width // HD
    heads = width // HD // groups
    total = rows * parts
    scale = HD ** (-0.5)
    pair = 2

    def kernel(p_ref, q_ref, o_ref, *rest):
        v_refs, k_refs = rest[:parts], rest[parts : 2 * parts]
        q_buf, o_buf, s_buf = rest[2 * parts :]

        @pl.loop(0, groups)
        def _(group):
            cols = lanes(group * HD, HD)
            stack_heads(group, heads, q_ref, q_buf)
            stack_heads(group, heads, o_ref, o_buf)
            for h in range(0, heads, pair):
                span = slice(h * rows, (h + pair) * rows)
                o = o_buf[span, :]
                grads, offset = [], 0.0
                for k in range(parts):
                    grad = lax.dot_general(v_refs[k][:, cols], o, NT, preferred_element_type=F32)
                    weight = p_ref[group, k * rows : (k + 1) * rows, span].astype(F32)
                    offset = offset + jnp.sum(weight * grad, axis=0, keepdims=True)
                    grads.append(grad)
                for k in range(parts):
                    weight = p_ref[group, k * rows : (k + 1) * rows, span].astype(F32)
                    s_buf[k * rows : (k + 1) * rows, span] = (weight * (grads[k] - offset)).astype(BF16)
            for k in range(parts):
                part = jnp.dot(s_buf[k * rows : (k + 1) * rows, :], q_buf[...], preferred_element_type=F32)
                k_refs[k][:, cols] = (part * scale).astype(k_refs[k].dtype)

    kinds = [F32] + [BF16] * (parts - 1)
    return pl.pallas_call(
        kernel,
        out_shape=[jax.ShapeDtypeStruct((rows, kv_width), kind) for kind in kinds],
        in_specs=[VMEM] * (3 + parts),
        out_specs=[VMEM] * parts,
        scratch_shapes=[pltpu.VMEM((heads * rows, HD), BF16)] * 2
        + [pltpu.VMEM((total, heads * rows), BF16)],
        compiler_params=grant(8 + 3 * parts),
        cost_estimate=estimate(4 * rows * total * width, 2 * (2 * rows * width + 2 * total * kv_width)),
        name="key_side",
    )(weights, queries, out_grads, *values)


def settle(parts_list):
    rows, cols = parts_list[0].shape

    def kernel(*refs):
        total = refs[0][...].astype(F32)
        for r in refs[1:-1]:
            total = total + r[...].astype(F32)
        refs[-1][...] = total.T.astype(BF16)

    return pl.pallas_call(
        kernel,
        out_shape=jax.ShapeDtypeStruct((cols, rows), BF16),
        in_specs=[VMEM] * len(parts_list),
        out_specs=VMEM,
        compiler_params=grant(8),
        cost_estimate=estimate(rows * cols * 4, 10 * rows * cols),
        name="settle",
    )(*parts_list)


def doc_grad(place, value_grads, features, spans, before, blocks, kind):
    parts = len(value_grads)
    rows = features[0][0].shape[0]
    chunk = sum(size for _, size in spans)
    cols = value_grads[0].shape[0]
    width = cols // blocks
    half = blocks // 2
    count = parts * len(spans)

    def kernel(place_ref, *refs):
        x_refs, d_refs = refs[:count], refs[count : count + parts]
        keep_ref, send_ref, square_ref = refs[-3:]
        odd = place_ref[2]

        def picked(which):
            blocks_of = []
            for z in range(half):
                block = pl.ds(pl.multiple_of((2 * z + which) * width, width), width)
                blocks_of.append(jnp.concatenate([r[block, :] for r in d_refs], axis=1))
            return jnp.concatenate(blocks_of, axis=0)

        ours, theirs = picked(odd), picked(1 - odd)
        squares = refs[count + parts][...]
        at = 0
        for i, (start, size) in enumerate(spans):
            span = slice(start, start + size)
            x = jnp.concatenate([r[:, span] for r in x_refs[i * parts : (i + 1) * parts]], axis=0)
            kept = jnp.dot(ours, x, preferred_element_type=F32)
            sent = jnp.dot(theirs, x, preferred_element_type=F32)
            keep_ref[:, at : at + size] = kept.astype(kind)
            send_ref[:, at : at + size] = sent.astype(BF16)
            both = kept * kept + sent * sent
            folded = jnp.sum(both.reshape(half * width // 8, 8, size), axis=0)
            for j in range(size // HD):
                squares = squares + folded[:, j * HD : (j + 1) * HD]
            at += size
        square_ref[...] = squares

    inputs = [x for chunk_of in features for x in chunk_of]
    return pl.pallas_call(
        kernel,
        out_shape=[
            jax.ShapeDtypeStruct((half * width, chunk), kind),
            jax.ShapeDtypeStruct((half * width, chunk), BF16),
            jax.ShapeDtypeStruct((8, HD), F32),
        ],
        in_specs=[SMEM] + [VMEM] * (count + parts + 1),
        out_specs=[VMEM] * 3,
        compiler_params=grant(10),
        cost_estimate=estimate(2 * rows * parts * chunk * cols, 2 * rows * parts * (chunk + cols) + 3 * cols * chunk),
        name="doc_grad",
    )(place, *inputs, *value_grads, before)


def pack(place, kept, received, blocks):
    half = blocks // 2
    tall, chunk = kept.shape
    width = tall // half

    def kernel(place_ref, keep_ref, got_ref, *outs):
        for k in range(half):
            rows = pl.ds(pl.multiple_of((place_ref[3] ^ k) * width, width), width)
            outs[k][:width, :] = keep_ref[rows, :]
            outs[k][width:, :] = got_ref[rows, :]

    return pl.pallas_call(
        kernel,
        out_shape=[jax.ShapeDtypeStruct((2 * width, chunk), BF16)] * half,
        in_specs=[SMEM, VMEM, VMEM],
        out_specs=[VMEM] * half,
        compiler_params=grant(8),
        cost_estimate=estimate(0, 8 * tall * chunk),
        name="pack",
    )(place, kept, received)


def finish(place, flag, own, plain, mine, first, others):
    planes = len(plain)
    width = plain[0].shape[0] // 2
    chunk = plain[0].shape[1]
    rest = mine.shape[1] - LANES

    def kernel(place_ref, own_ref, *refs):
        plain_refs, (mine_ref, *got_refs, out_ref, held, sems) = refs[:planes], refs[planes:]
        factors = [[own_ref[:1, :1], own_ref[8:9, :1]]]
        sums = mine_ref[:, :rest].astype(F32)
        if flag is None:
            for r in got_refs:
                factors.append(gather_terms(r[:TERMS, rest:]))
                sums = sums + r[:, :rest].astype(F32)
        else:
            first_ref, far_ref, near_ref, last_ref = got_refs
            inner = place_ref[flag] == 1
            factors.append(gather_terms(first_ref[:TERMS, rest:]))
            last = last_ref[: 2 * TERMS, rest:]
            for ref, start in ((far_ref, 0), (near_ref, TERMS)):
                direct = gather_terms(ref[:TERMS, rest:])
                passed = gather_terms(last[start : start + TERMS])
                factors.append([jnp.where(inner, d, p) for d, p in zip(direct, passed)])
            for r in got_refs[1:]:
                sums = sums + r[:, :rest].astype(F32)
            got = first_ref[:, :rest].astype(F32)
            sums = sums + jnp.where(inner, jnp.zeros_like(got), got)
        held[:, chunk:] = sums
        back = pltpu.make_async_copy(held.at[:, pl.ds(chunk, rest)], out_ref.at[:, pl.ds(chunk, rest)], sems.at[0])
        back.start()
        total = 0.0
        for (even, odd), r in zip(factors, plain_refs):
            total = total + r[:width, :].astype(F32) * even + r[width:, :].astype(F32) * odd
        held[:, :chunk] = total
        front = pltpu.make_async_copy(held.at[:, pl.ds(0, chunk)], out_ref.at[:, pl.ds(0, chunk)], sems.at[1])
        front.start()
        back.wait()
        front.wait()

    args = [own, *plain, mine, first, *others]
    return pl.pallas_call(
        kernel,
        out_shape=jax.ShapeDtypeStruct((width, chunk + rest), F32),
        in_specs=[SMEM] + [VMEM] * len(args),
        out_specs=pl.BlockSpec(memory_space=pl.ANY),
        scratch_shapes=[pltpu.VMEM((width, chunk + rest), F32), pltpu.SemaphoreType.DMA((2,))],
        compiler_params=grant(8),
        cost_estimate=estimate(12 * width * (chunk + rest), 20 * width * (chunk + rest)),
        name="finish",
    )(place, *args)


def spread(value):
    rest = jnp.broadcast_to(value, (1, LANES))
    terms = []
    for _ in range(3):
        term = rest.astype(BF16)
        rest = rest - term.astype(F32)
        terms.append(term)
    return terms + [jnp.zeros((1, LANES), BF16)]


def gather_terms(block):
    block = block.astype(F32)
    return [block[i : i + 1, :1] + block[i + 1 : i + 2, :1] + block[i + 2 : i + 3, :1] for i in (0, 4)]


def combine(place, squares, kept, received, order, blocks, clip):
    half = blocks // 2
    tall = kept[0].shape[0]
    sizes = [k.shape[1] for k in kept]
    whole = sum(sizes)
    width = tall // half
    chunks = len(kept)
    count = len(squares)

    def kernel(place_ref, *refs):
        square_refs = refs[:count]
        keep_refs = refs[count : count + chunks]
        got_refs = refs[count + chunks : count + 2 * chunks]
        norm_ref, factor_ref = refs[count + 2 * chunks : count + 2 * chunks + 2]
        outs = refs[count + 2 * chunks + 2 :]
        sums = square_refs[0][...]
        for r in square_refs[1:]:
            sums = sums + r[...]

        def norm(block):
            lanes = jnp.sum(block, axis=1, keepdims=True)
            return jnp.sqrt(jnp.sum(lanes, axis=0, keepdims=True))

        mine, other = norm(sums[:8]), norm(sums[8:])
        norm_ref[...] = jnp.broadcast_to(mine, (8, HD))
        mine, other = clip / (mine + 0.01), clip / (other + 0.01)
        factor_ref[:8, :] = jnp.broadcast_to(mine, (8, HD))
        factor_ref[8:, :] = jnp.broadcast_to(other, (8, HD))
        terms = jnp.concatenate(spread(mine) + spread(other), axis=0)
        for i in range(half):
            outs[i][:TERMS, whole:] = terms
            outs[i][TERMS:, whole:] = jnp.zeros((width - TERMS, LANES), BF16)
            rows = pl.ds(pl.multiple_of(place_ref[order + i] * width, width), width)
            for j in range(chunks):
                total = keep_refs[j][rows, :] * mine + got_refs[j][rows, :].astype(F32) * other
                start = sum(sizes[:j])
                outs[i][:, start : start + sizes[j]] = total.astype(BF16)

    out = pl.pallas_call(
        kernel,
        out_shape=[jax.ShapeDtypeStruct((8, HD), F32), jax.ShapeDtypeStruct((16, HD), F32)]
        + [jax.ShapeDtypeStruct((width, whole + LANES), BF16)] * half,
        in_specs=[SMEM] + [VMEM] * (count + 2 * chunks),
        out_specs=[VMEM] * (half + 2),
        compiler_params=grant(12),
        cost_estimate=estimate(4 * tall * whole, 8 * tall * whole),
        name="combine",
    )(place, *squares, *kept, *received)
    return out[0], out[1], out[2:]


def relay(place, flag, mine, got):
    whole = mine.shape[1] - LANES

    def kernel(place_ref, mine_ref, got_ref, out_ref):
        got = got_ref[:, :whole].astype(F32)
        got = jnp.where(place_ref[flag] == 1, got, jnp.zeros_like(got))
        out_ref[:, :whole] = (mine_ref[:, :whole].astype(F32) + got).astype(BF16)
        out_ref[:, whole:] = mine_ref[:, whole:]
        out_ref[TERMS : 2 * TERMS, whole:] = got_ref[:TERMS, whole:]

    return pl.pallas_call(
        kernel,
        out_shape=jax.ShapeDtypeStruct(mine.shape, BF16),
        in_specs=[SMEM, VMEM, VMEM],
        out_specs=VMEM,
        compiler_params=grant(8),
        cost_estimate=estimate(2 * mine.size, 6 * mine.size),
        name="relay",
    )(place, mine, got)


def add_up(place, flag, gated, terms, kind):
    def kernel(place_ref, *refs):
        total = refs[len(gated)][...].astype(F32)
        for r in refs[len(gated) + 1 : -1]:
            total = total + r[...].astype(F32)
        for r in refs[: len(gated)]:
            got = r[...].astype(F32)
            total = total + jnp.where(place_ref[flag] == 1, jnp.zeros_like(got), got)
        refs[-1][...] = total.astype(kind)

    size = terms[0].size
    return pl.pallas_call(
        kernel,
        out_shape=jax.ShapeDtypeStruct(terms[0].shape, kind),
        in_specs=[SMEM] + [VMEM] * (len(gated) + len(terms)),
        out_specs=VMEM,
        compiler_params=grant(8),
        cost_estimate=estimate(8 * size, 14 * size),
        name="add_up",
    )(place, *gated, *terms)


def step(layer_input, value_weight, queries, key_states, out_grads, lengths):
    parts = lax.axis_size("context")
    docs = lax.axis_size("dp")
    planes = docs // 2
    context = lax.axis_index("context")
    doc = lax.axis_index("dp")
    z = doc // 2
    if planes == 4:
        order = [z, 3 * (1 - z % 2), 2 - z // 2]
        order.append(6 - sum(order))
    else:
        order = [z ^ k for k in range(planes)]
    inner = (z > 0) & (z < planes - 1)
    place = jnp.stack([context, lengths[0], doc % 2, z, inner] + order).astype(jnp.int32)
    width = layer_input.shape[2]
    sizes = split(width // parts)
    early = max(1, width // parts // LANES * EARLY_SHARE // 16) * LANES
    spans = [(early, sizes[0] - early), (0, sizes[1])]
    start = 0 if early < sizes[0] else 1
    spans = spans[start:]
    cols = value_weight.shape[1]

    def over_context(x, k):
        return lax.ppermute(x, "context", [(i, i ^ k) for i in range(parts)])

    def over_planes(x, hops):
        return lax.ppermute(x, "dp", [(2 * a + c, 2 * b + c) for a, b in hops for c in range(2)])

    def swap(k):
        return [(i, i ^ k) for i in range(planes)]

    def over_cores(x):
        return lax.ppermute(x, "dp", [(i, i ^ 1) for i in range(docs)])

    zeros = anchor()
    keys = [over_context(key_states[0], k) for k in range(1, parts)]
    pieces, grads, heads = cut(place, layer_input[0], out_grads[0], queries[0], parts, sizes)
    features = []
    for j in range(len(sizes)):
        features.append([pieces[0][j]] + [over_context(pieces[k][j], k) for k in range(1, parts)])
    own_keys = key_states[0] * (lengths[0] >= 0).astype(BF16)
    weights, value_parts = weigh(place, heads, grads, [own_keys] + keys)
    blocks = [value_parts[0]] + [over_context(value_parts[k], k) for k in range(1, parts)]
    value_low = settle(blocks)
    value_grads = [value_low] + [over_context(value_low, k) for k in range(1, parts)]

    keep, send, square = doc_grad(place, value_grads, features[:1], [(0, early)], zeros, docs, BF16)
    got = over_cores(send)
    plain = pack(place, keep, got, docs)
    plain = [plain[0]] + [over_planes(plain[k], swap(k)) for k in range(1, planes)]
    keep, send, square = doc_grad(place, value_grads, features[start:], spans, square, docs, F32)
    got = over_cores(send)
    squares = jnp.concatenate([square, over_cores(square)], axis=0)
    squares = [squares] + [over_context(squares, k) for k in range(1, parts)]
    norm, factors, shares = combine(place, squares, [keep], [got], 5, docs, math.sqrt(width * cols))


    own_values = project(layer_input[0], value_weight)
    values = [own_values] + [over_context(own_values, k) for k in range(1, parts)]
    key_parts = key_side(weights, heads, grads, values)
    key_blocks = [key_parts[0]] + [over_context(key_parts[k], k) for k in range(1, parts)]
    key_grads = add_up(place, 4, [], key_blocks, BF16)[None]

    if planes == 4:
        first = over_planes(shares[1], [(0, 1), (1, 0), (2, 3), (3, 2)])
        far = over_planes(shares[2], [(0, 2), (3, 1)])
        near = over_planes(shares[2], [(1, 2), (2, 1)])
        onward = relay(place, 4, shares[3], first)
        last = over_planes(onward, [(0, 1), (3, 2), (1, 3), (2, 0)])
        total = finish(place, 4, factors, plain, shares[0], first, [far, near, last])
    else:
        got = [over_planes(shares[k], swap(k)) for k in range(1, planes)]
        total = finish(place, None, factors, plain, shares[0], got[0], got[1:])
    return total.T, norm[0, :1], key_grads


def solution(mesh):
    placed = (
        P("dp", "context", None),
        P(),
        P("dp", "context", None),
        P("dp", "context", None),
        P("dp", "context", None),
        P("dp"),
    )
    return jax.shard_map(
        step,
        mesh=mesh,
        in_specs=placed,
        out_specs=(P("context", "dp"), P("dp"), P("dp", "context", None)),
        check_vma=False,
    )
```

```python
import math

import jax
import jax.numpy as jnp
from jax import lax
from jax.experimental import pallas as pl
from jax.experimental.pallas import tpu as pltpu
from jax.sharding import PartitionSpec as P

HD = 128
LANES = 128
TERMS = 8
EARLY_SHARE = 6
FIRST_SHARE = 8
HEAVY = 10
F32 = jnp.float32
BF16 = jnp.bfloat16
LOG2E = 1.4426950408889634


NT = (((1,), (1,)), ((), ()))
VMEM = pl.BlockSpec(memory_space=pltpu.VMEM)
SMEM = pl.BlockSpec(memory_space=pltpu.SMEM)


def estimate(flops, nbytes, exps=0):
    return pl.CostEstimate(flops=flops, bytes_accessed=nbytes, transcendentals=exps)


def grant(mib):
    return pltpu.CompilerParams(vmem_limit_bytes=mib << 20)


def split(own):
    units = own // LANES
    first = max(1, units * FIRST_SHARE // 16)
    return [first * LANES, (units - first) * LANES]


def cut(place, layer_rows, out_grads, queries, parts, sizes):
    rows, width = layer_rows.shape
    own = width // parts
    chunks = len(sizes)
    heads = out_grads.shape[1]

    def kernel(place_ref, x_ref, o_ref, q_ref, *refs):
        outs, (grad_ref, query_ref) = refs[: parts * chunks], refs[parts * chunks :]
        for k in range(parts):
            start = (place_ref[0] ^ k) * own
            for j in range(chunks):
                span = pl.ds(pl.multiple_of(start + sum(sizes[:j]), LANES), sizes[j])
                outs[k * chunks + j][...] = x_ref[:, span]
        me, length = place_ref[0], place_ref[1]
        valid = me * rows + lax.broadcasted_iota(jnp.int32, (rows, LANES), 0) < length
        for start in range(0, heads, LANES):
            block = o_ref[:, start : start + LANES]
            grad_ref[:, start : start + LANES] = jnp.where(valid, block, jnp.zeros_like(block))
        query_ref[...] = q_ref[...]

    out = pl.pallas_call(
        kernel,
        out_shape=[jax.ShapeDtypeStruct((rows, size), BF16) for _ in range(parts) for size in sizes]
        + [jax.ShapeDtypeStruct(out_grads.shape, BF16)] * 2,
        in_specs=[SMEM] + [VMEM] * 3,
        out_specs=[VMEM] * (parts * chunks + 2),
        compiler_params=grant(12),
        cost_estimate=estimate(0, HEAVY * 4 * rows * width),
        name="cut",
    )(place, layer_rows, out_grads, queries)
    return [[out[k * chunks + j] for j in range(chunks)] for k in range(parts)], *out[-2:]


def anchor():
    def kernel(out_ref):
        out_ref[...] = jnp.zeros((8, HD), F32)

    return pl.pallas_call(
        kernel,
        out_shape=jax.ShapeDtypeStruct((8, HD), F32),
        out_specs=VMEM,
        compiler_params=grant(1),
        cost_estimate=estimate(10**10, 0),
        name="anchor",
    )()


def project(layer_rows, value_weight):
    rows, width = layer_rows.shape
    cols = value_weight.shape[1]
    depth = 2048

    def kernel(x_ref, w_ref, v_ref):
        total = jnp.zeros((rows, cols), F32)
        for start in range(0, width, depth):
            span = slice(start, start + depth)
            total = total + jnp.dot(x_ref[:, span], w_ref[span, :], preferred_element_type=F32)
        v_ref[...] = total.astype(BF16)

    return pl.pallas_call(
        kernel,
        out_shape=jax.ShapeDtypeStruct((rows, cols), BF16),
        in_specs=[VMEM, VMEM],
        out_specs=VMEM,
        compiler_params=grant(14),
        cost_estimate=estimate(2 * rows * width * cols, 2 * width * (cols + rows)),
        name="project",
    )(layer_rows, value_weight)


def lanes(start, size):
    return pl.ds(pl.multiple_of(start, size), size)


def stack_heads(group, heads, source, target):
    rows = source.shape[0]
    for h in range(heads):
        target[h * rows : (h + 1) * rows, :] = source[:, lanes((group * heads + h) * HD, HD)]


def weigh(place, queries, out_grads, keys):
    rows, width = queries.shape
    parts = len(keys)
    kv_width = keys[0].shape[1]
    groups = kv_width // HD
    heads = width // HD // groups
    total = rows * parts
    factor = HD ** (-0.5) * LOG2E
    pair = 2

    def kernel(place_ref, q_ref, o_ref, *rest):
        k_refs, p_ref = rest[:parts], rest[parts]
        v_refs, (q_buf, o_buf) = rest[parts + 1 : 2 * parts + 1], rest[2 * parts + 1 :]
        me = place_ref[0]
        row = lax.broadcasted_iota(jnp.int32, (rows, pair * rows), 0)
        lane = lax.broadcasted_iota(jnp.int32, (rows, pair * rows), 1)
        causal = row <= lax.rem(lane, rows)

        @pl.loop(0, groups)
        def _(group):
            cols = lanes(group * HD, HD)
            stack_heads(group, heads, q_ref, q_buf)
            stack_heads(group, heads, o_ref, o_buf)
            for h in range(0, heads, pair):
                span = slice(h * rows, (h + pair) * rows)
                q = q_buf[span, :]
                scores = [lax.dot_general(r[:, cols], q, NT, preferred_element_type=F32) for r in k_refs]
                scores[0] = jnp.where(causal, scores[0], -jnp.inf)
                peak = jnp.max(scores[0], axis=0, keepdims=True)
                for k in range(1, parts):
                    higher = jnp.maximum(peak, jnp.max(scores[k], axis=0, keepdims=True))
                    peak = jnp.where((me ^ k) < me, higher, peak)
                peak = peak * factor
                sums = 0.0
                for k in range(parts):
                    shift = peak if k == 0 else jnp.where((me ^ k) < me, peak, jnp.inf)
                    scores[k] = jnp.exp2(scores[k] * factor - shift)
                    sums = sums + jnp.sum(scores[k], axis=0, keepdims=True)
                inverse = 1.0 / sums
                for k in range(parts):
                    p_ref[group, k * rows : (k + 1) * rows, span] = (scores[k] * inverse).astype(BF16)
            for k in range(parts):
                block = p_ref[group, k * rows : (k + 1) * rows, :]
                part = jnp.dot(block, o_buf[...], preferred_element_type=F32)
                v_refs[k][:, cols] = part.astype(v_refs[k].dtype)

    kinds = [F32] + [BF16] * (parts - 1)
    out = pl.pallas_call(
        kernel,
        out_shape=[jax.ShapeDtypeStruct((groups, total, heads * rows), BF16)]
        + [jax.ShapeDtypeStruct((rows, kv_width), kind) for kind in kinds],
        in_specs=[SMEM] + [VMEM] * (2 + parts),
        out_specs=[VMEM] * (1 + parts),
        scratch_shapes=[pltpu.VMEM((heads * rows, HD), BF16)] * 2,
        compiler_params=grant(8 + 2 * parts),
        cost_estimate=estimate(
            HEAVY * 4 * rows * total * width,
            2 * (2 * rows * width + 2 * total * kv_width),
            rows * total * width // HD,
        ),
        name="weigh",
    )(place, queries, out_grads, *keys)
    return out[0], out[1:]


def key_side(weights, queries, out_grads, values):
    rows, width = queries.shape
    parts = len(values)
    kv_width = values[0].shape[1]
    groups = kv_width // HD
    heads = width // HD // groups
    total = rows * parts
    scale = HD ** (-0.5)
    pair = 2

    def kernel(p_ref, q_ref, o_ref, *rest):
        v_refs, k_refs = rest[:parts], rest[parts : 2 * parts]
        q_buf, o_buf, s_buf = rest[2 * parts :]

        @pl.loop(0, groups)
        def _(group):
            cols = lanes(group * HD, HD)
            stack_heads(group, heads, q_ref, q_buf)
            stack_heads(group, heads, o_ref, o_buf)
            for h in range(0, heads, pair):
                span = slice(h * rows, (h + pair) * rows)
                o = o_buf[span, :]
                grads, offset = [], 0.0
                for k in range(parts):
                    grad = lax.dot_general(v_refs[k][:, cols], o, NT, preferred_element_type=F32)
                    weight = p_ref[group, k * rows : (k + 1) * rows, span].astype(F32)
                    offset = offset + jnp.sum(weight * grad, axis=0, keepdims=True)
                    grads.append(grad)
                for k in range(parts):
                    weight = p_ref[group, k * rows : (k + 1) * rows, span].astype(F32)
                    s_buf[k * rows : (k + 1) * rows, span] = (weight * (grads[k] - offset)).astype(BF16)
            for k in range(parts):
                part = jnp.dot(s_buf[k * rows : (k + 1) * rows, :], q_buf[...], preferred_element_type=F32)
                k_refs[k][:, cols] = (part * scale).astype(k_refs[k].dtype)

    kinds = [F32] + [BF16] * (parts - 1)
    return pl.pallas_call(
        kernel,
        out_shape=[jax.ShapeDtypeStruct((rows, kv_width), kind) for kind in kinds],
        in_specs=[VMEM] * (3 + parts),
        out_specs=[VMEM] * parts,
        scratch_shapes=[pltpu.VMEM((heads * rows, HD), BF16)] * 2
        + [pltpu.VMEM((total, heads * rows), BF16)],
        compiler_params=grant(8 + 3 * parts),
        cost_estimate=estimate(4 * rows * total * width, 2 * (2 * rows * width + 2 * total * kv_width)),
        name="key_side",
    )(weights, queries, out_grads, *values)


def settle(parts_list):
    rows, cols = parts_list[0].shape

    def kernel(*refs):
        total = refs[0][...].astype(F32)
        for r in refs[1:-1]:
            total = total + r[...].astype(F32)
        refs[-1][...] = total.T.astype(BF16)

    return pl.pallas_call(
        kernel,
        out_shape=jax.ShapeDtypeStruct((cols, rows), BF16),
        in_specs=[VMEM] * len(parts_list),
        out_specs=VMEM,
        compiler_params=grant(8),
        cost_estimate=estimate(rows * cols * 4, 10 * rows * cols),
        name="settle",
    )(*parts_list)


def doc_grad(place, value_grads, features, spans, before, blocks, kind):
    parts = len(value_grads)
    rows = features[0][0].shape[0]
    chunk = sum(size for _, size in spans)
    cols = value_grads[0].shape[0]
    width = cols // blocks
    half = blocks // 2
    count = parts * len(spans)

    def kernel(place_ref, *refs):
        x_refs, d_refs = refs[:count], refs[count : count + parts]
        keep_ref, send_ref, square_ref = refs[-3:]
        odd = place_ref[2]

        def picked(which):
            blocks_of = []
            for z in range(half):
                block = pl.ds(pl.multiple_of((2 * z + which) * width, width), width)
                blocks_of.append(jnp.concatenate([r[block, :] for r in d_refs], axis=1))
            return jnp.concatenate(blocks_of, axis=0)

        ours, theirs = picked(odd), picked(1 - odd)
        squares = refs[count + parts][...]
        at = 0
        for i, (start, size) in enumerate(spans):
            span = slice(start, start + size)
            x = jnp.concatenate([r[:, span] for r in x_refs[i * parts : (i + 1) * parts]], axis=0)
            kept = jnp.dot(ours, x, preferred_element_type=F32)
            sent = jnp.dot(theirs, x, preferred_element_type=F32)
            keep_ref[:, at : at + size] = kept.astype(kind)
            send_ref[:, at : at + size] = sent.astype(BF16)
            both = kept * kept + sent * sent
            folded = jnp.sum(both.reshape(half * width // 8, 8, size), axis=0)
            for j in range(size // HD):
                squares = squares + folded[:, j * HD : (j + 1) * HD]
            at += size
        square_ref[...] = squares

    inputs = [x for chunk_of in features for x in chunk_of]
    return pl.pallas_call(
        kernel,
        out_shape=[
            jax.ShapeDtypeStruct((half * width, chunk), kind),
            jax.ShapeDtypeStruct((half * width, chunk), BF16),
            jax.ShapeDtypeStruct((8, HD), F32),
        ],
        in_specs=[SMEM] + [VMEM] * (count + parts + 1),
        out_specs=[VMEM] * 3,
        compiler_params=grant(10),
        cost_estimate=estimate(2 * rows * parts * chunk * cols, 2 * rows * parts * (chunk + cols) + 3 * cols * chunk),
        name="doc_grad",
    )(place, *inputs, *value_grads, before)


def pack(place, kept, received, blocks):
    half = blocks // 2
    tall, chunk = kept.shape
    width = tall // half

    def kernel(place_ref, keep_ref, got_ref, *outs):
        for k in range(half):
            rows = pl.ds(pl.multiple_of((place_ref[3] ^ k) * width, width), width)
            outs[k][:width, :] = keep_ref[rows, :]
            outs[k][width:, :] = got_ref[rows, :]

    return pl.pallas_call(
        kernel,
        out_shape=[jax.ShapeDtypeStruct((2 * width, chunk), BF16)] * half,
        in_specs=[SMEM, VMEM, VMEM],
        out_specs=[VMEM] * half,
        compiler_params=grant(8),
        cost_estimate=estimate(0, 8 * tall * chunk),
        name="pack",
    )(place, kept, received)


def finish(place, flag, own, plain, mine, first, others):
    planes = len(plain)
    width = plain[0].shape[0] // 2
    chunk = plain[0].shape[1]
    rest = mine.shape[1] - LANES

    def pieces(size):
        step = 3 * LANES
        return [(at, min(step, size - at)) for at in range(0, size, step)]

    count = len(pieces(rest)) + len(pieces(chunk))

    def kernel(place_ref, own_ref, *refs):
        plain_refs, (mine_ref, *got_refs, out_ref, held, sems) = refs[:planes], refs[planes:]
        copies = []

        def put(start, size, value):
            held[:, start : start + size] = value
            span = pl.ds(start, size)
            copy = pltpu.make_async_copy(held.at[:, span], out_ref.at[:, span], sems.at[len(copies)])
            copy.start()
            copies.append(copy)

        factors = [[own_ref[:1, :1], own_ref[8:9, :1]]]
        if flag is None:
            inner, added = None, got_refs
            for r in got_refs:
                factors.append(gather_terms(r[:TERMS, rest:]))
        else:
            first_ref, far_ref, near_ref, last_ref = got_refs
            inner, added = place_ref[flag] == 1, got_refs[1:]
            factors.append(gather_terms(first_ref[:TERMS, rest:]))
            last = last_ref[: 2 * TERMS, rest:]
            for ref, start in ((far_ref, 0), (near_ref, TERMS)):
                direct = gather_terms(ref[:TERMS, rest:])
                passed = gather_terms(last[start : start + TERMS])
                factors.append([jnp.where(inner, d, p) for d, p in zip(direct, passed)])
        for at, size in pieces(rest):
            span = slice(at, at + size)
            sums = mine_ref[:, span].astype(F32)
            for r in added:
                sums = sums + r[:, span].astype(F32)
            if flag is not None:
                got = got_refs[0][:, span].astype(F32)
                sums = sums + jnp.where(inner, jnp.zeros_like(got), got)
            put(chunk + at, size, sums)
        for at, size in pieces(chunk):
            span = slice(at, at + size)
            total = 0.0
            for (even, odd), r in zip(factors, plain_refs):
                total = total + r[:width, span].astype(F32) * even + r[width:, span].astype(F32) * odd
            put(at, size, total)
        for copy in copies:
            copy.wait()

    args = [own, *plain, mine, first, *others]
    return pl.pallas_call(
        kernel,
        out_shape=jax.ShapeDtypeStruct((width, chunk + rest), F32),
        in_specs=[SMEM] + [VMEM] * len(args),
        out_specs=pl.BlockSpec(memory_space=pl.ANY),
        scratch_shapes=[pltpu.VMEM((width, chunk + rest), F32), pltpu.SemaphoreType.DMA((count,))],
        compiler_params=grant(8),
        cost_estimate=estimate(12 * width * (chunk + rest), 20 * width * (chunk + rest)),
        name="finish",
    )(place, *args)


def spread(value):
    rest = jnp.broadcast_to(value, (1, LANES))
    terms = []
    for _ in range(3):
        term = rest.astype(BF16)
        rest = rest - term.astype(F32)
        terms.append(term)
    return terms + [jnp.zeros((1, LANES), BF16)]


def gather_terms(block):
    block = block.astype(F32)
    return [block[i : i + 1, :1] + block[i + 1 : i + 2, :1] + block[i + 2 : i + 3, :1] for i in (0, 4)]


def combine(place, squares, kept, received, order, blocks, clip):
    half = blocks // 2
    tall = kept[0].shape[0]
    sizes = [k.shape[1] for k in kept]
    whole = sum(sizes)
    width = tall // half
    chunks = len(kept)
    count = len(squares)

    def kernel(place_ref, *refs):
        square_refs = refs[:count]
        keep_refs = refs[count : count + chunks]
        got_refs = refs[count + chunks : count + 2 * chunks]
        norm_ref, factor_ref = refs[count + 2 * chunks : count + 2 * chunks + 2]
        outs = refs[count + 2 * chunks + 2 :]
        sums = square_refs[0][...]
        for r in square_refs[1:]:
            sums = sums + r[...]

        def norm(block):
            lanes = jnp.sum(block, axis=1, keepdims=True)
            return jnp.sqrt(jnp.sum(lanes, axis=0, keepdims=True))

        mine, other = norm(sums[:8]), norm(sums[8:])
        norm_ref[...] = jnp.broadcast_to(mine, (8, HD))
        mine, other = clip / (mine + 0.01), clip / (other + 0.01)
        factor_ref[:8, :] = jnp.broadcast_to(mine, (8, HD))
        factor_ref[8:, :] = jnp.broadcast_to(other, (8, HD))
        terms = jnp.concatenate(spread(mine) + spread(other), axis=0)
        for i in range(half):
            outs[i][:TERMS, whole:] = terms
            outs[i][TERMS:, whole:] = jnp.zeros((width - TERMS, LANES), BF16)
            rows = pl.ds(pl.multiple_of(place_ref[order + i] * width, width), width)
            for j in range(chunks):
                total = keep_refs[j][rows, :] * mine + got_refs[j][rows, :].astype(F32) * other
                start = sum(sizes[:j])
                outs[i][:, start : start + sizes[j]] = total.astype(BF16)

    out = pl.pallas_call(
        kernel,
        out_shape=[jax.ShapeDtypeStruct((8, HD), F32), jax.ShapeDtypeStruct((16, HD), F32)]
        + [jax.ShapeDtypeStruct((width, whole + LANES), BF16)] * half,
        in_specs=[SMEM] + [VMEM] * (count + 2 * chunks),
        out_specs=[VMEM] * (half + 2),
        compiler_params=grant(12),
        cost_estimate=estimate(4 * tall * whole, 8 * tall * whole),
        name="combine",
    )(place, *squares, *kept, *received)
    return out[0], out[1], out[2:]


def relay(place, flag, mine, got):
    whole = mine.shape[1] - LANES

    def kernel(place_ref, mine_ref, got_ref, out_ref):
        got = got_ref[:, :whole].astype(F32)
        got = jnp.where(place_ref[flag] == 1, got, jnp.zeros_like(got))
        out_ref[:, :whole] = (mine_ref[:, :whole].astype(F32) + got).astype(BF16)
        out_ref[:, whole:] = mine_ref[:, whole:]
        out_ref[TERMS : 2 * TERMS, whole:] = got_ref[:TERMS, whole:]

    return pl.pallas_call(
        kernel,
        out_shape=jax.ShapeDtypeStruct(mine.shape, BF16),
        in_specs=[SMEM, VMEM, VMEM],
        out_specs=VMEM,
        compiler_params=grant(8),
        cost_estimate=estimate(2 * mine.size, 6 * mine.size),
        name="relay",
    )(place, mine, got)


def add_up(place, flag, gated, terms, kind):
    def kernel(place_ref, *refs):
        total = refs[len(gated)][...].astype(F32)
        for r in refs[len(gated) + 1 : -1]:
            total = total + r[...].astype(F32)
        for r in refs[: len(gated)]:
            got = r[...].astype(F32)
            total = total + jnp.where(place_ref[flag] == 1, jnp.zeros_like(got), got)
        refs[-1][...] = total.astype(kind)

    size = terms[0].size
    return pl.pallas_call(
        kernel,
        out_shape=jax.ShapeDtypeStruct(terms[0].shape, kind),
        in_specs=[SMEM] + [VMEM] * (len(gated) + len(terms)),
        out_specs=VMEM,
        compiler_params=grant(8),
        cost_estimate=estimate(8 * size, 14 * size),
        name="add_up",
    )(place, *gated, *terms)


def step(layer_input, value_weight, queries, key_states, out_grads, lengths):
    parts = lax.axis_size("context")
    docs = lax.axis_size("dp")
    planes = docs // 2
    context = lax.axis_index("context")
    doc = lax.axis_index("dp")
    z = doc // 2
    if planes == 4:
        order = [z, 3 * (1 - z % 2), 2 - z // 2]
        order.append(6 - sum(order))
    else:
        order = [z ^ k for k in range(planes)]
    inner = (z > 0) & (z < planes - 1)
    place = jnp.stack([context, lengths[0], doc % 2, z, inner] + order).astype(jnp.int32)
    width = layer_input.shape[2]
    sizes = split(width // parts)
    early = max(1, width // parts // LANES * EARLY_SHARE // 16) * LANES
    spans = [(early, sizes[0] - early), (0, sizes[1])]
    start = 0 if early < sizes[0] else 1
    spans = spans[start:]
    cols = value_weight.shape[1]

    def over_context(x, k):
        return lax.ppermute(x, "context", [(i, i ^ k) for i in range(parts)])

    def over_planes(x, hops):
        return lax.ppermute(x, "dp", [(2 * a + c, 2 * b + c) for a, b in hops for c in range(2)])

    def swap(k):
        return [(i, i ^ k) for i in range(planes)]

    def over_cores(x):
        return lax.ppermute(x, "dp", [(i, i ^ 1) for i in range(docs)])

    zeros = anchor()
    keys = [over_context(key_states[0], k) for k in range(1, parts)]
    pieces, grads, heads = cut(place, layer_input[0], out_grads[0], queries[0], parts, sizes)
    features = []
    for j in range(len(sizes)):
        features.append([pieces[0][j]] + [over_context(pieces[k][j], k) for k in range(1, parts)])
    own_keys = key_states[0] * (lengths[0] >= 0).astype(BF16)
    weights, value_parts = weigh(place, heads, grads, [own_keys] + keys)
    blocks = [value_parts[0]] + [over_context(value_parts[k], k) for k in range(1, parts)]
    value_low = settle(blocks)
    value_grads = [value_low] + [over_context(value_low, k) for k in range(1, parts)]

    keep, send, square = doc_grad(place, value_grads, features[:1], [(0, early)], zeros, docs, BF16)
    got = over_cores(send)
    plain = pack(place, keep, got, docs)
    plain = [plain[0]] + [over_planes(plain[k], swap(k)) for k in range(1, planes)]
    keep, send, square = doc_grad(place, value_grads, features[start:], spans, square, docs, F32)
    got = over_cores(send)
    squares = jnp.concatenate([square, over_cores(square)], axis=0)
    squares = [squares] + [over_context(squares, k) for k in range(1, parts)]
    norm, factors, shares = combine(place, squares, [keep], [got], 5, docs, math.sqrt(width * cols))


    own_values = project(layer_input[0], value_weight)
    values = [own_values] + [over_context(own_values, k) for k in range(1, parts)]
    key_parts = key_side(weights, heads, grads, values)
    key_blocks = [key_parts[0]] + [over_context(key_parts[k], k) for k in range(1, parts)]
    key_grads = add_up(place, 4, [], key_blocks, BF16)[None]

    if planes == 4:
        first = over_planes(shares[1], [(0, 1), (1, 0), (2, 3), (3, 2)])
        far = over_planes(shares[2], [(0, 2), (3, 1)])
        near = over_planes(shares[2], [(1, 2), (2, 1)])
        onward = relay(place, 4, shares[3], first)
        last = over_planes(onward, [(0, 1), (3, 2), (1, 3), (2, 0)])
        total = finish(place, 4, factors, plain, shares[0], first, [far, near, last])
    else:
        got = [over_planes(shares[k], swap(k)) for k in range(1, planes)]
        total = finish(place, None, factors, plain, shares[0], got[0], got[1:])
    return total.T, norm[0, :1], key_grads


def solution(mesh):
    placed = (
        P("dp", "context", None),
        P(),
        P("dp", "context", None),
        P("dp", "context", None),
        P("dp", "context", None),
        P("dp"),
    )
    return jax.shard_map(
        step,
        mesh=mesh,
        in_specs=placed,
        out_specs=(P("context", "dp"), P("dp"), P("dp", "context", None)),
        check_vma=False,
    )
```
